256 devices in a mesh: gx: 32 (over y, x, core), gz: 8 (over z).
Axes of the slice: x: 4, y: 4, z: 8, core: 2. Of those that a mesh axis runs over, the one named last changes fastest.
Arguments:
- velocity: float32 [64, 3, 128, 64, 256], P(None, None, 'gx', 'gz'), may hold values from -40 to 40
- scaled_modes: float32 [64, 128, 64, 256], P(None, 'gx', 'gz'), may hold values from -70 to 70
Outputs:
- orthonormal: float32 [128, 128, 64, 256], P(None, 'gx', 'gz')
- triangle: float32 [128, 128], replicated
- lower_one: float32 [128, 128], replicated
The draws below stay inside these ranges and needn't reach their ends.
All inputs are finite; a program needn't handle non-finite values.
Results may differ from the reference program's by a relative error of at most 0.0003.
Values sent between devices are 32-bit elements; how exact they have to be, the bound alone decides.
No kernel may reach another device: no remote copies, remote signals or barrier semaphores. Data moves between devices by JAX's collectives and lax.ppermute only.
A program may use at most 128 MiB of HBM per device.

```python
import math
import jax
import jax.numpy as jnp
from jax import lax

MODES = 64
SNAP = 64
NY = 256
COLS = 128
NX = 128
NZ = 64


def streamwise_scale(key, lowest, highest):
    position = jnp.arange(NX, dtype=jnp.float32) / NX
    rough = jax.random.uniform(key, (NX,), jnp.float32, math.log(lowest), math.log(highest))
    return jnp.exp(math.log(3.0) * position + rough)


def draw_velocity(key, part):
    first_key, second_key, third_key = jax.random.split(key, 3)
    shape = (SNAP, 3, NX, NZ, NY)
    noise = jnp.clip(jax.random.normal(first_key, shape, jnp.float32), -4.0, 4.0)
    plane = streamwise_scale(second_key, 0.6, 1.6)
    amplitude = jnp.exp(jax.random.uniform(third_key, (SNAP,), jnp.float32, math.log(0.5), math.log(2.0)))
    flow = noise * plane[None, None, :, None, None] * amplitude[:, None, None, None, None]
    return flow


def draw_scaled_modes(key, part):
    first_key, second_key, third_key, fourth_key = jax.random.split(key, 4)
    shape = (MODES, NX, NZ, NY)
    groups = (MODES + 3) // 4
    shared_shape = (groups, NX, NZ, NY)
    noise = jnp.clip(jax.random.normal(first_key, shape, jnp.float32), -4.0, 4.0)
    shared = jnp.clip(jax.random.normal(fourth_key, shared_shape, jnp.float32), -4.0, 4.0)
    plane = streamwise_scale(second_key, 0.6, 1.6)
    spread = 0.02
    column = jnp.exp(jax.random.uniform(third_key, (MODES,), jnp.float32, math.log(0.3), math.log(3.0)))
    which_shared = jnp.arange(MODES, dtype=jnp.int32) // 4
    mixed = shared[which_shared] + spread * noise
    return mixed * plane[None, :, None, None] * column[:, None, None, None]


def setup_inputs(seed: int = 0) -> dict:
    streams_of = jax.random.split(jax.random.key(seed), 3)
    velocity = draw_velocity(jax.random.fold_in(streams_of[2], 71), 0)
    scaled_modes = draw_scaled_modes(jax.random.fold_in(streams_of[2], 71), 0)
    return dict(velocity=velocity, scaled_modes=scaled_modes)


precise = lax.Precision.HIGHEST

def central(field, along):
    return (jnp.roll(field, -1, along) - jnp.roll(field, 1, along)) * 0.5

def along_wall(field):
    inner = (field[..., 2:] - field[..., :-2]) * 0.5
    bottom = (-3.0 * field[..., 0:1] + 4.0 * field[..., 1:2] - field[..., 2:3]) * 0.5
    top_side = (3.0 * field[..., -1:] - 4.0 * field[..., -2:-1] + field[..., -3:-2]) * 0.5
    return jnp.concatenate([bottom, inner, top_side], -1)

def criterion(flow):
    grad_x = central(flow, 1)
    grad_z = central(flow, 2)
    grad_y = along_wall(flow)
    diagonal_part = grad_x[0] * grad_x[0] + grad_z[1] * grad_z[1] + grad_y[2] * grad_y[2]
    cross_part = grad_z[0] * grad_x[1] + grad_y[0] * grad_x[2] + grad_y[1] * grad_z[2]
    return -0.5 * diagonal_part - cross_part

def product(left, right):
    return lax.dot_general(left, right, (((1,), (1,)), ((), ())), precision=precise)

def reference(velocity, scaled_modes):
    fields = lax.map(criterion, velocity)
    total_cells = NX * NZ * NY
    stacked = jnp.concatenate([scaled_modes.reshape(MODES, -1), fields.reshape(SNAP, -1)], 0)
    lower_one = jnp.linalg.cholesky(product(stacked, stacked) / total_cells)
    first_pass = lax.linalg.triangular_solve(lower_one, stacked, left_side=True, lower=True)
    lower_two = jnp.linalg.cholesky(product(first_pass, first_pass) / total_cells)
    basis = lax.linalg.triangular_solve(lower_two, first_pass, left_side=True, lower=True)
    triangle = jnp.dot(lower_two.T, lower_one.T, precision=precise)
    return (basis.reshape(COLS, NX, NZ, NY), triangle, lower_one)
```

```python
import jax
import jax.numpy as jnp
from jax import lax
from jax.sharding import PartitionSpec as P

precise = lax.Precision.HIGHEST


def with_halo(block, sides, width):
    for axis, dim in sides:
        count = lax.axis_size(axis)
        forward = [(i, i + 1) for i in range(count - 1)]
        forward.append((count - 1, 0))
        backward = [(target, source) for source, target in forward]
        low = lax.ppermute(
            lax.slice_in_dim(block, block.shape[dim] - width, None, axis=dim), axis, forward
        )
        high = lax.ppermute(lax.slice_in_dim(block, 0, width, axis=dim), axis, backward)
        block = jnp.concatenate([low, block, high], axis=dim)
    return block


def along_wall(field):
    inner = (field[..., 2:] - field[..., :-2]) * 0.5
    bottom = (-3.0 * field[..., 0:1] + 4.0 * field[..., 1:2] - field[..., 2:3]) * 0.5
    top_side = (3.0 * field[..., -1:] - 4.0 * field[..., -2:-1] + field[..., -3:-2]) * 0.5
    return jnp.concatenate([bottom, inner, top_side], -1)


def product(left, right):
    return lax.dot_general(left, right, (((1,), (1,)), ((), ())), precision=precise)


def all_sum(value):
    size_x, size_z = lax.axis_size("gx"), lax.axis_size("gz")
    flips = [(1 << bit, 0) for bit in range(size_x.bit_length() - 1)]
    flips += [(0, 1 << bit) for bit in range(size_z.bit_length() - 1)]
    for flip_x, flip_z in flips:
        pairs = [
            (x * size_z + z, (x ^ flip_x) * size_z + (z ^ flip_z))
            for x in range(size_x)
            for z in range(size_z)
        ]
        value = value + lax.ppermute(value, ("gx", "gz"), pairs)
    return value


def shards(velocity, scaled_modes):
    snapshots, _, cells_x, cells_z, cells_y = velocity.shape
    columns_old = scaled_modes.shape[0]
    total_cells = cells_x * lax.axis_size("gx") * cells_z * lax.axis_size("gz") * cells_y
    mode_fields = scaled_modes.reshape(columns_old, -1)
    padded = with_halo(velocity, (("gx", 2), ("gz", 3)), 1)
    grad_x = (padded[:, :, 2:, 1:-1] - padded[:, :, :-2, 1:-1]) * 0.5
    grad_z = (padded[:, :, 1:-1, 2:] - padded[:, :, 1:-1, :-2]) * 0.5
    grad_y = along_wall(velocity)
    diagonal_part = (
        grad_x[:, 0] * grad_x[:, 0] + grad_z[:, 1] * grad_z[:, 1] + grad_y[:, 2] * grad_y[:, 2]
    )
    cross_part = (
        grad_z[:, 0] * grad_x[:, 1] + grad_y[:, 0] * grad_x[:, 2] + grad_y[:, 1] * grad_z[:, 2]
    )
    new_fields = (-0.5 * diagonal_part - cross_part).reshape(snapshots, -1)
    stacked = jnp.concatenate([mode_fields, new_fields], 0)
    gram_sum = all_sum(product(stacked, stacked))
    lower_one = jnp.linalg.cholesky(gram_sum / total_cells)
    first_pass = lax.linalg.triangular_solve(lower_one, stacked, left_side=True, lower=True)
    second_sum = all_sum(product(first_pass, first_pass))
    lower_two = jnp.linalg.cholesky(second_sum / total_cells)
    basis = lax.linalg.triangular_solve(lower_two, first_pass, left_side=True, lower=True)
    triangle = jnp.dot(lower_two.T, lower_one.T, precision=precise)
    return (basis.reshape(stacked.shape[0], cells_x, cells_z, cells_y), triangle, lower_one)


def solution(mesh):
    in_specs = (P(None, None, "gx", "gz", None), P(None, "gx", "gz", None))
    out_specs = (P(None, "gx", "gz", None), P(), P())
    return jax.shard_map(shards, mesh=mesh, in_specs=in_specs, out_specs=out_specs, check_vma=False)
```

```python
import jax
import jax.numpy as jnp
from jax import lax
from jax.experimental import pallas as pl
from jax.experimental.pallas import tpu as pltpu
from jax.sharding import PartitionSpec as P

precise = lax.Precision.HIGHEST
LANES = 128


def pack_faces(velocity, group=16):
    snaps, comps, nx, nz, ny = velocity.shape
    halves = ny // LANES
    rows = group * comps * nx

    def kernel(*refs):
        views, (first_x, last_x, first_z, last_z) = refs[:halves], refs[halves:]
        for h, v_ref in enumerate(views):
            lanes = slice(h * LANES, (h + 1) * LANES)
            first_x[:, :, :, lanes] = v_ref[:, :, 0]
            last_x[:, :, :, lanes] = v_ref[:, :, nx - 1]
            flat = v_ref.reshape(rows * nz, LANES)
            first_z[h] = flat[pl.ds(0, rows, stride=nz), :]
            last_z[h] = flat[pl.ds(nz - 1, rows, stride=nz), :]

    face_x = jax.ShapeDtypeStruct((snaps, comps, nz, ny), velocity.dtype)
    face_z = jax.ShapeDtypeStruct((halves, snaps * comps * nx, LANES), velocity.dtype)
    spec_x = pl.BlockSpec((group, comps, nz, ny), lambda i: (i, 0, 0, 0))
    spec_z = pl.BlockSpec((halves, rows, LANES), lambda i: (0, i, 0))
    block = (group, comps, nx, nz, LANES)
    return pl.pallas_call(
        kernel,
        grid=(snaps // group,),
        in_specs=[pl.BlockSpec(block, lambda i, h=h: (i, 0, 0, 0, h)) for h in range(halves)],
        out_specs=[spec_x, spec_x, spec_z, spec_z],
        out_shape=[face_x, face_x, face_z, face_z],
        name="pack_faces",
    )(*[velocity] * halves)


def flatten_modes(modes, group=2):
    count, nx, nz, ny = modes.shape
    halves = ny // LANES

    def kernel(*refs):
        out_ref = refs[halves]
        for h in range(halves):
            flat = refs[h].reshape(count * group * nz, LANES)
            for x in range(group):
                for z in range(nz):
                    start = ((x * halves + h) * nz + z) * LANES
                    out_ref[:, start : start + LANES] = flat[pl.ds(x * nz + z, count, stride=group * nz), :]

    block = (count, group, nz, LANES)
    return pl.pallas_call(
        kernel,
        grid=(nx // group,),
        in_specs=[pl.BlockSpec(block, lambda i, h=h: (0, i, 0, h)) for h in range(halves)],
        out_specs=pl.BlockSpec((count, group * nz * ny), lambda i: (0, i)),
        out_shape=jax.ShapeDtypeStruct((count, nx * nz * ny), modes.dtype),
        name="flatten_modes",
    )(*[modes] * halves)


def criterion(velocity, low_x, high_x, low_z, high_z, group=8):
    snaps, comps, nx, nz, ny = velocity.shape
    rows = group * comps * nx
    halves = ny // LANES

    def kernel(v_ref, lx_ref, hx_ref, lz_ref, hz_ref, out_ref, q_ref):
        lane = lax.broadcasted_iota(jnp.int32, (nz, LANES), 1)
        level = lax.broadcasted_iota(jnp.int32, (nz, LANES), 0)

        def cut(half):
            return slice(half * LANES, (half + 1) * LANES)

        def wall(parts):
            below = [pltpu.roll(p, 1, 1) for p in parts]
            above = [pltpu.roll(p, LANES - 1, 1) for p in parts]
            out = []
            for h in range(halves):
                fm = jnp.where(lane == 0, below[h - 1], below[h]) if h else below[h]
                fp = jnp.where(lane == LANES - 1, above[h + 1], above[h]) if h < halves - 1 else above[h]
                d = fp - fm
                if h == 0:
                    d = jnp.where(lane == 0, -3.0 * parts[h] + 4.0 * fp - pltpu.roll(parts[h], LANES - 2, 1), d)
                if h == halves - 1:
                    d = jnp.where(lane == LANES - 1, 3.0 * parts[h] - 4.0 * fm + pltpu.roll(parts[h], 2, 1), d)
                out.append(d)
            return out

        def body(s, carry):
            for x in range(nx):
                dx, dz, dy = [], [], []
                for c in range(comps):
                    here = [v_ref[s, c, x, :, cut(h)] for h in range(halves)]
                    dx.append([
                        (v_ref[s, c, x + 1, :, cut(h)] if x < nx - 1 else hx_ref[s, c, :, cut(h)])
                        - (v_ref[s, c, x - 1, :, cut(h)] if x else lx_ref[s, c, :, cut(h)])
                        for h in range(halves)
                    ])
                    row = (s * comps + c) * nx + x
                    part = []
                    for h in range(halves):
                        up = jnp.where(level == nz - 1, hz_ref.at[h][pl.ds(row, nz, stride=0), :], pltpu.roll(here[h], nz - 1, 0))
                        down = jnp.where(level == 0, lz_ref.at[h][pl.ds(row, nz, stride=0), :], pltpu.roll(here[h], 1, 0))
                        part.append(up - down)
                    dz.append(part)
                    dy.append(wall(here))
                for h in range(halves):
                    diagonal = dx[0][h] * dx[0][h] + dz[1][h] * dz[1][h] + dy[2][h] * dy[2][h]
                    cross = dz[0][h] * dx[1][h] + dy[0][h] * dx[2][h] + dy[1][h] * dz[2][h]
                    q_ref[h, pl.ds((s * nx + x) * nz, nz), :] = -0.125 * diagonal - 0.25 * cross
            return carry

        lax.fori_loop(0, group, body, 0)
        for x in range(nx):
            for z in range(nz):
                for h in range(halves):
                    start = ((x * halves + h) * nz + z) * LANES
                    view = q_ref.at[h]
                    out_ref[:, start : start + LANES] = view[pl.ds(x * nz + z, group, stride=nx * nz), :]

    spec_x = pl.BlockSpec((group, comps, nz, ny), lambda i: (i, 0, 0, 0))
    spec_z = pl.BlockSpec((halves, rows, LANES), lambda i: (0, i, 0))
    return pl.pallas_call(
        kernel,
        grid=(snaps // group,),
        in_specs=[pl.BlockSpec((group, comps, nx, nz, ny), lambda i: (i, 0, 0, 0, 0)), spec_x, spec_x, spec_z, spec_z],
        out_specs=pl.BlockSpec((group, nx * nz * ny), lambda i: (i, 0)),
        out_shape=jax.ShapeDtypeStruct((snaps, nx * nz * ny), velocity.dtype),
        scratch_shapes=[pltpu.VMEM((halves, group * nx * nz, LANES), velocity.dtype)],
        name="criterion",
    )(velocity, low_x, high_x, low_z, high_z)


def spread(row, shape):
    return jnp.broadcast_to(row, shape)


def three_parts(value):
    first = value.astype(jnp.bfloat16).astype(jnp.float32)
    rest = value - first
    second = rest.astype(jnp.bfloat16).astype(jnp.float32)
    return first, second, rest - second


def eliminate(a_ref, x_ref, u_ref):
    size = a_ref.shape[0]
    tall = 8
    row = lax.broadcasted_iota(jnp.int32, (tall, size), 0)
    lane = lax.broadcasted_iota(jnp.int32, (tall, size), 1)
    full = (tall, size)
    full_row = lax.broadcasted_iota(jnp.int32, (size, size), 0)
    full_lane = lax.broadcasted_iota(jnp.int32, (size, size), 1)
    x_ref[...] = jnp.where(full_row == full_lane, 1.0, 0.0)
    for start in range(0, size, tall):
        rows = slice(start, start + tall)
        left, right = a_ref[rows, :], x_ref[rows, :]
        columns = [spread(left[:, start + j : start + j + 1], full) for j in range(tall)]
        pivots = jnp.ones(full, jnp.float32)
        for j in range(tall):
            pivot = spread(columns[j][j : j + 1, :], full)
            pivots = jnp.where(row == j, pivot, pivots)
            if j == tall - 1:
                break
            factor = jnp.where(row > j, columns[j] * (1.0 / pivot), 0.0)
            for k in range(j + 1, tall):
                columns[k] = columns[k] - factor * spread(columns[k][j : j + 1, :], full)
            left = left - factor * spread(left[j : j + 1, :], full)
            right = right - factor * spread(right[j : j + 1, :], full)
        scale = 1.0 / jnp.sqrt(pivots)
        left = jnp.where(lane >= start + row, left * scale, 0.0)
        right = right * scale
        u_ref[rows, :] = left
        x_ref[rows, :] = right
        if start + tall < size:
            l1, l2, l3 = three_parts(left)
            r1, r2, r3 = three_parts(right)
            lhs = jnp.concatenate([l1, l1, l2, l2, l1, l3], 0).astype(jnp.bfloat16)
            rhs_left = jnp.concatenate([l1, l2, l1, l2, l3, l1], 0).astype(jnp.bfloat16)
            rhs_right = jnp.concatenate([r1, r2, r1, r2, r3, r1], 0).astype(jnp.bfloat16)
            rhs = jnp.concatenate([rhs_left, rhs_right], 1)
            change = lax.dot_general(lhs, rhs, (((0,), (0,)), ((), ())), preferred_element_type=jnp.float32)
            below = slice(start + tall, size)
            a_ref[below, :] -= change[start + tall :, :size]
            x_ref[below, :] -= change[start + tall :, size:]


def matmul(left, right, dims=((1,), (0,))):
    return lax.dot_general(left, right, (dims, ((), ())), precision=precise, preferred_element_type=jnp.float32)


def split(value, top):
    big = top * (1.5 * 2.0**16)
    first = (value + big) - big
    rest = value - first
    second = rest.astype(jnp.bfloat16).astype(jnp.float32)
    rest = rest - second
    third = rest.astype(jnp.bfloat16).astype(jnp.float32)
    return first, second, third, rest - third


def residual(gram, upper):
    parts = [p.astype(jnp.bfloat16) for p in split(upper, jnp.max(jnp.abs(upper), 0, keepdims=True))]

    def cross(i, j):
        return lax.dot_general(parts[i], parts[j], (((0,), (0,)), ((), ())), preferred_element_type=jnp.float32)

    out = gram - cross(0, 0)
    both = cross(1, 0)
    out = out - (both + both.T)
    both = cross(2, 0) + (cross(3, 0) + cross(2, 1))
    return out - (cross(1, 1) + (both + both.T))


def factor(mine, other, core, cells):
    size = mine.shape[2]
    half = size // 2
    quarter = half // 2

    def kernel(core_ref, mine_ref, other_ref, weight_ref, triangle_ref, lower_ref, a_ref, x_ref, u_ref, y_ref, v_ref):
        full_row = lax.broadcasted_iota(jnp.int32, (size, size), 0)
        full_lane = lax.broadcasted_iota(jnp.int32, (size, size), 1)
        first = core_ref[0] == 0

        def whole(k):
            low = jnp.where(first, mine_ref[k], other_ref[k])
            high = jnp.where(first, other_ref[k], mine_ref[k])
            corner = jnp.concatenate([low[quarter:], high[quarter:]], 0)
            rows = jnp.concatenate([low[:quarter], high[:quarter], pltpu.roll(corner, half, 1), corner], 0)
            rows = rows * (1.0 / cells)
            return jnp.where(full_lane >= full_row, rows, rows.T)

        gram, extra = whole(0), whole(1)
        a_ref[...] = gram
        eliminate(a_ref, x_ref, u_ref)
        upper = u_ref[...]
        eye = jnp.where(full_row == full_lane, 1.0, 0.0)
        inverse = refined(x_ref[...], upper, eye)
        lower_ref[...] = upper.T
        rest = residual(gram, upper) + extra
        change = matmul(matmul(inverse, rest), inverse, ((1,), (1,)))
        change = jnp.where(full_lane <= full_row, change, change.T)
        small = jnp.sum(change * change) < 2.0**-18

        @pl.when(small)
        def _():
            keep = jnp.where(full_lane < full_row, 1.0, jnp.where(full_lane == full_row, 0.5, 0.0))
            step = keep * change
            step = keep * (change - matmul(step, step, ((1,), (1,))))
            weight_ref[...] = inverse - matmul(step, inverse - matmul(step, inverse))
            triangle_ref[...] = upper + matmul(step, upper, ((0,), (0,)))

        @pl.when(jnp.logical_not(small))
        def _():
            a_ref[...] = change + eye
            eliminate(a_ref, y_ref, v_ref)
            weight_ref[...] = matmul(refined(y_ref[...], v_ref[...], eye), inverse)
            triangle_ref[...] = matmul(v_ref[...], upper)

    square = jax.ShapeDtypeStruct((size, size), jnp.float32)
    vmem = pl.BlockSpec(memory_space=pltpu.VMEM)
    return pl.pallas_call(
        kernel,
        in_specs=[pl.BlockSpec(memory_space=pltpu.SMEM), vmem, vmem],
        out_specs=[vmem, vmem, vmem],
        out_shape=[square, square, square],
        scratch_shapes=[pltpu.VMEM((size, size), jnp.float32)] * 5,
        name="factor",
    )(core, mine, other)


def refined(inverse, upper, eye):
    return inverse + matmul(eye - matmul(inverse, upper, ((1,), (1,))), inverse)


def two_sum(left, right):
    total = left + right
    back = total - left
    return total, (left - (total - back)) + (right - back)


def gram_halves(modes, fields, core, chunk=2048, piece=512):
    old, cells = modes.shape
    new = fields.shape[0]
    size = old + new
    half, quarter = size // 2, size // 4
    steps = cells // chunk

    def kernel(core_ref, m_ref, f_ref, keep_ref, send_ref, high_ref, low_ref, cross_ref):
        step = pl.program_id(0)

        @pl.when(step == 0)
        def _():
            high_ref[...] = jnp.zeros_like(high_ref)
            low_ref[...] = jnp.zeros_like(low_ref)
            cross_ref[...] = jnp.zeros_like(cross_ref)

        for k in range(chunk // piece):
            span = slice(k * piece, (k + 1) * piece)
            block = jnp.concatenate([m_ref[:, span], f_ref[:, span]], 0)
            first, second, third, _ = split(block, jnp.max(jnp.abs(block), 1, keepdims=True))
            lhs = jnp.concatenate([first, second, third], 0).astype(jnp.bfloat16)
            part = lax.dot_general(
                lhs, lhs[: 2 * size], (((1,), (1,)), ((), ())), preferred_element_type=jnp.float32
            )
            high_ref[...], error = two_sum(high_ref[...], part[:size, :size])
            low_ref[...] += error + part[size : 2 * size, size:]
            cross_ref[...] += part[size : 2 * size, :size] + (part[2 * size :, :size] + part[2 * size :, size:])

        @pl.when(step == steps - 1)
        def _():
            cross = cross_ref[...]
            high_ref[...], low_ref[...] = two_sum(high_ref[...], low_ref[...] + (cross + cross.T))
            lane = lax.broadcasted_iota(jnp.int32, (quarter, size), 1)
            lead = core_ref[0] == 0
            for k, ref in enumerate((high_ref, low_ref)):
                corner = jnp.where(lane < half, pltpu.roll(ref[half : half + quarter, :], half, 1), ref[half + quarter :, :])
                low = jnp.concatenate([ref[:quarter, :], corner[: quarter // 2]], 0)
                high = jnp.concatenate([ref[quarter:half, :], corner[quarter // 2 :]], 0)
                keep_ref[k] = jnp.where(lead, low, high)
                send_ref[k] = jnp.where(lead, high, low)

    out = jax.ShapeDtypeStruct((2, quarter + quarter // 2, size), jnp.float32)
    spec = pl.BlockSpec((2, quarter + quarter // 2, size), lambda i: (0, 0, 0))
    return pl.pallas_call(
        kernel,
        grid=(steps,),
        in_specs=[
            pl.BlockSpec(memory_space=pltpu.SMEM),
            pl.BlockSpec((old, chunk), lambda i: (0, i)),
            pl.BlockSpec((new, chunk), lambda i: (0, i)),
        ],
        out_specs=[spec, spec],
        out_shape=[out, out],
        scratch_shapes=[pltpu.VMEM((size, size), jnp.float32)] * 3,
        name="gram_halves",
    )(core, modes, fields)


def apply_split(weight, modes, fields, nx, nz, ny):
    old, cells = modes.shape
    new = fields.shape[0]
    count = old + new
    halves = ny // LANES

    def kernel(w_ref, m_ref, f_ref, out_ref):
        w1, w2, w3 = three_parts(w_ref[...])
        lhs = jnp.concatenate(
            [
                jnp.concatenate([w1, w2], 1),
                jnp.concatenate([w2, w1], 1),
                jnp.concatenate([w3, jnp.zeros_like(w3)], 1),
            ],
            0,
        ).astype(jnp.bfloat16)
        block = jnp.concatenate([m_ref[...], f_ref[...]], 0)
        s1, s2, s3 = three_parts(block)
        pair = jnp.concatenate([s1, s2], 0).astype(jnp.bfloat16)
        dims = (((1,), (0,)), ((), ()))
        main = lax.dot_general(lhs, pair, dims, preferred_element_type=jnp.float32)
        tail = lax.dot_general(w1.astype(jnp.bfloat16), s3.astype(jnp.bfloat16), dims, preferred_element_type=jnp.float32)
        result = main[:count] + (main[count : 2 * count] + (main[2 * count :] + tail))
        flat = out_ref.reshape(count * nz, LANES)
        for z in range(nz):
            flat[pl.ds(z, count, stride=nz), :] = result[:, z * LANES : (z + 1) * LANES]

    return pl.pallas_call(
        kernel,
        grid=(nx, halves),
        in_specs=[
            pl.BlockSpec((count, count), lambda i, h: (0, 0)),
            pl.BlockSpec((old, nz * LANES), lambda i, h: (0, i * halves + h)),
            pl.BlockSpec((new, nz * LANES), lambda i, h: (0, i * halves + h)),
        ],
        out_specs=pl.BlockSpec((count, 1, nz, LANES), lambda i, h: (0, i, 0, h)),
        out_shape=jax.ShapeDtypeStruct((count, nx, nz, ny), jnp.float32),
        name="apply_split",
    )(weight, modes, fields)


def shifted(value, axis, forward):
    count = lax.axis_size(axis)
    step = 1 if forward else count - 1
    return lax.ppermute(value, axis, [(i, (i + step) % count) for i in range(count)])


def flipped(value, flip_x, flip_z):
    size_x, size_z = lax.axis_size("gx"), lax.axis_size("gz")
    pairs = [
        (x * size_z + z, (x ^ flip_x) * size_z + (z ^ flip_z)) for x in range(size_x) for z in range(size_z)
    ]
    return lax.ppermute(value, ("gx", "gz"), pairs)


def pair_sum(left, right):
    high, error = two_sum(left[0], right[0])
    return jnp.stack([high, left[1] + right[1] + error])


def all_sum(keep, send):
    value = pair_sum(keep, flipped(send, 1, 0))
    flips = [(1 << bit, 0) for bit in range(1, lax.axis_size("gx").bit_length() - 1)]
    flips += [(0, 1 << bit) for bit in range(lax.axis_size("gz").bit_length() - 1)]
    for flip_x, flip_z in flips:
        value = pair_sum(value, flipped(value, flip_x, flip_z))
    return value, flipped(value, 1, 0)


def shards(velocity, scaled_modes):
    _, _, cells_x, cells_z, cells_y = velocity.shape
    total_cells = cells_x * lax.axis_size("gx") * cells_z * lax.axis_size("gz") * cells_y
    core = (lax.axis_index("gx") % 2).astype(jnp.int32).reshape(1)
    first_x, last_x, first_z, last_z = pack_faces(velocity)
    low_x, high_x = shifted(last_x, "gx", True), shifted(first_x, "gx", False)
    low_z, high_z = shifted(last_z, "gz", True), shifted(first_z, "gz", False)
    modes = flatten_modes(scaled_modes)
    fields = criterion(velocity, low_x, high_x, low_z, high_z)
    mine, other = all_sum(*gram_halves(modes, fields, core))
    weight, triangle, lower_one = factor(mine, other, core, float(total_cells))
    basis = apply_split(weight, modes, fields, cells_x, cells_z, cells_y)
    return basis, triangle, lower_one


def solution(mesh):
    in_specs = (P(None, None, "gx", "gz", None), P(None, "gx", "gz", None))
    out_specs = (P(None, "gx", "gz", None), P(), P())
    return jax.shard_map(shards, mesh=mesh, in_specs=in_specs, out_specs=out_specs, check_vma=False)
```

```python
import jax
import jax.numpy as jnp
from jax import lax
from jax.experimental import pallas as pl
from jax.experimental.pallas import tpu as pltpu
from jax.sharding import PartitionSpec as P

precise = lax.Precision.HIGHEST
LANES = 128
SPANS = ((0, 32), (32, 32))


def pack_faces(velocity, begin, snaps, group=16):
    _, comps, nx, nz, ny = velocity.shape
    skip = begin // group
    halves = ny // LANES
    rows = group * comps * nx

    def kernel(*refs):
        views, (first_x, last_x, first_z, last_z) = refs[:halves], refs[halves:]
        for h, v_ref in enumerate(views):
            lanes = slice(h * LANES, (h + 1) * LANES)
            first_x[:, :, :, lanes] = v_ref[:, :, 0]
            last_x[:, :, :, lanes] = v_ref[:, :, nx - 1]
            flat = v_ref.reshape(rows * nz, LANES)
            first_z[h] = flat[pl.ds(0, rows, stride=nz), :]
            last_z[h] = flat[pl.ds(nz - 1, rows, stride=nz), :]

    face_x = jax.ShapeDtypeStruct((snaps, comps, nz, ny), velocity.dtype)
    face_z = jax.ShapeDtypeStruct((halves, snaps * comps * nx, LANES), velocity.dtype)
    spec_x = pl.BlockSpec((group, comps, nz, ny), lambda i: (i, 0, 0, 0))
    spec_z = pl.BlockSpec((halves, rows, LANES), lambda i: (0, i, 0))
    block = (group, comps, nx, nz, LANES)
    return pl.pallas_call(
        kernel,
        grid=(snaps // group,),
        in_specs=[pl.BlockSpec(block, lambda i, h=h: (i + skip, 0, 0, 0, h)) for h in range(halves)],
        out_specs=[spec_x, spec_x, spec_z, spec_z],
        out_shape=[face_x, face_x, face_z, face_z],
        name="pack_faces",
    )(*[velocity] * halves)


def flatten_modes(modes, group=2):
    count, nx, nz, ny = modes.shape
    halves = ny // LANES

    def kernel(*refs):
        out_ref = refs[halves]
        for h in range(halves):
            flat = refs[h].reshape(count * group * nz, LANES)
            for x in range(group):
                for z in range(nz):
                    start = ((x * halves + h) * nz + z) * LANES
                    out_ref[:, start : start + LANES] = flat[pl.ds(x * nz + z, count, stride=group * nz), :]

    block = (count, group, nz, LANES)
    return pl.pallas_call(
        kernel,
        grid=(nx // group,),
        in_specs=[pl.BlockSpec(block, lambda i, h=h: (0, i, 0, h)) for h in range(halves)],
        out_specs=pl.BlockSpec((count, group * nz * ny), lambda i: (0, i)),
        out_shape=jax.ShapeDtypeStruct((count, nx * nz * ny), modes.dtype),
        name="flatten_modes",
    )(*[modes] * halves)


def criterion(velocity, low_x, high_x, low_z, high_z, begin, group=8):
    _, comps, nx, nz, ny = velocity.shape
    snaps = low_x.shape[0]
    skip = begin // group
    halves = ny // LANES

    def kernel(v_ref, lx_ref, hx_ref, lz_ref, hz_ref, out_ref, q_ref):
        lane = lax.broadcasted_iota(jnp.int32, (nz, LANES), 1)
        level = lax.broadcasted_iota(jnp.int32, (nz, LANES), 0)

        def cut(half):
            return slice(half * LANES, (half + 1) * LANES)

        def wall(parts):
            below = [pltpu.roll(p, 1, 1) for p in parts]
            above = [pltpu.roll(p, LANES - 1, 1) for p in parts]
            out = []
            for h in range(halves):
                here = parts[h]
                fp = jnp.where(lane == LANES - 1, above[h + 1], above[h]) if h < halves - 1 else above[h]
                if h:
                    fm = jnp.where(lane == 0, below[h - 1], below[h])
                else:
                    edge = 3.0 * (here - fp) + pltpu.roll(here, LANES - 2, 1)
                    fm = jnp.where(lane == 0, edge, below[h])
                if h == halves - 1:
                    edge = 3.0 * (here - fm) + pltpu.roll(here, 2, 1)
                    fp = jnp.where(lane == LANES - 1, edge, fp)
                d = fp - fm
                out.append(d)
            return out

        def body(s, carry):
            t = pl.program_id(0) * group + s
            for x in range(nx):
                dx, dz, dy = [], [], []
                for c in range(comps):
                    here = [v_ref[s, c, x, :, cut(h)] for h in range(halves)]
                    dx.append([
                        (v_ref[s, c, x + 1, :, cut(h)] if x < nx - 1 else hx_ref[t, c, :, cut(h)])
                        - (v_ref[s, c, x - 1, :, cut(h)] if x else lx_ref[t, c, :, cut(h)])
                        for h in range(halves)
                    ])
                    row = (t * comps + c) * nx + x
                    part = []
                    for h in range(halves):
                        up = jnp.where(level == nz - 1, hz_ref.at[h][pl.ds(row, nz, stride=0), :], pltpu.roll(here[h], nz - 1, 0))
                        down = jnp.where(level == 0, lz_ref.at[h][pl.ds(row, nz, stride=0), :], pltpu.roll(here[h], 1, 0))
                        part.append(up - down)
                    dz.append(part)
                    dy.append(wall(here))
                for h in range(halves):
                    diagonal = dx[0][h] * dx[0][h] + dz[1][h] * dz[1][h] + dy[2][h] * dy[2][h]
                    cross = dz[0][h] * dx[1][h] + dy[0][h] * dx[2][h] + dy[1][h] * dz[2][h]
                    q_ref[h, pl.ds((s * nx + x) * nz, nz), :] = -0.125 * diagonal - 0.25 * cross
            return carry

        lax.fori_loop(0, group, body, 0, unroll=4)
        for x in range(nx):
            for z in range(nz):
                for h in range(halves):
                    start = ((x * halves + h) * nz + z) * LANES
                    view = q_ref.at[h]
                    out_ref[:, start : start + LANES] = view[pl.ds(x * nz + z, group, stride=nx * nz), :]

    near = pl.BlockSpec(memory_space=pltpu.VMEM)
    return pl.pallas_call(
        kernel,
        grid=(snaps // group,),
        in_specs=[pl.BlockSpec((group, comps, nx, nz, ny), lambda i: (i + skip, 0, 0, 0, 0)), near, near, near, near],
        out_specs=pl.BlockSpec((group, nx * nz * ny), lambda i: (i, 0)),
        out_shape=jax.ShapeDtypeStruct((snaps, nx * nz * ny), velocity.dtype),
        scratch_shapes=[pltpu.VMEM((halves, group * nx * nz, LANES), velocity.dtype)],
        name="criterion",
    )(velocity, *[pltpu.with_memory_space_constraint(halo, pltpu.VMEM) for halo in (low_x, high_x, low_z, high_z)])


def spread(row, shape):
    return jnp.broadcast_to(row, shape)


def three_parts(value):
    first = value.astype(jnp.bfloat16).astype(jnp.float32)
    rest = value - first
    second = rest.astype(jnp.bfloat16).astype(jnp.float32)
    return first, second, rest - second


def eliminate(a_ref, x_ref, u_ref):
    size = a_ref.shape[0]
    tall = 8
    row = lax.broadcasted_iota(jnp.int32, (tall, size), 0)
    lane = lax.broadcasted_iota(jnp.int32, (tall, size), 1)
    full = (tall, size)
    full_row = lax.broadcasted_iota(jnp.int32, (size, size), 0)
    full_lane = lax.broadcasted_iota(jnp.int32, (size, size), 1)
    x_ref[...] = jnp.where(full_row == full_lane, 1.0, 0.0)
    for start in range(0, size, tall):
        rows = slice(start, start + tall)
        left, right = a_ref[rows, :], x_ref[rows, :]
        columns = [spread(left[:, start + j : start + j + 1], full) for j in range(tall)]
        pivots = jnp.ones(full, jnp.float32)
        for j in range(tall):
            pivot = spread(columns[j][j : j + 1, :], full)
            pivots = jnp.where(row == j, pivot, pivots)
            if j == tall - 1:
                break
            factor = jnp.where(row > j, columns[j] * (1.0 / pivot), 0.0)
            for k in range(j + 1, tall):
                columns[k] = columns[k] - factor * spread(columns[k][j : j + 1, :], full)
            left = left - factor * spread(left[j : j + 1, :], full)
            right = right - factor * spread(right[j : j + 1, :], full)
        scale = 1.0 / jnp.sqrt(pivots)
        left = jnp.where(lane >= start + row, left * scale, 0.0)
        right = right * scale
        u_ref[rows, :] = left
        x_ref[rows, :] = right
        if start + tall < size:
            l1, l2, l3 = three_parts(left)
            r1, r2, r3 = three_parts(right)
            lhs = jnp.concatenate([l1, l1, l2, l2, l1, l3], 0).astype(jnp.bfloat16)
            rhs_left = jnp.concatenate([l1, l2, l1, l2, l3, l1], 0).astype(jnp.bfloat16)
            rhs_right = jnp.concatenate([r1, r2, r1, r2, r3, r1], 0).astype(jnp.bfloat16)
            rhs = jnp.concatenate([rhs_left, rhs_right], 1)
            change = lax.dot_general(lhs, rhs, (((0,), (0,)), ((), ())), preferred_element_type=jnp.float32)
            below = slice(start + tall, size)
            a_ref[below, :] -= change[start + tall :, :size]
            x_ref[below, :] -= change[start + tall :, size:]


def matmul(left, right, dims=((1,), (0,))):
    return lax.dot_general(left, right, (dims, ((), ())), precision=precise, preferred_element_type=jnp.float32)


def split(value, top):
    big = top * (1.5 * 2.0**16)
    first = (value + big) - big
    rest = value - first
    second = rest.astype(jnp.bfloat16).astype(jnp.float32)
    rest = rest - second
    third = rest.astype(jnp.bfloat16).astype(jnp.float32)
    return first, second, third, rest - third


def residual(gram, upper):
    parts = [p.astype(jnp.bfloat16) for p in split(upper, jnp.max(jnp.abs(upper), 0, keepdims=True))]

    def cross(i, j):
        return lax.dot_general(parts[i], parts[j], (((0,), (0,)), ((), ())), preferred_element_type=jnp.float32)

    out = gram - cross(0, 0)
    both = cross(1, 0)
    out = out - (both + both.T)
    both = cross(2, 0) + (cross(3, 0) + cross(2, 1))
    return out - (cross(1, 1) + (both + both.T))


def factor(mine, other, core, cells):
    size = mine.shape[2]
    half = size // 2
    quarter = half // 2

    def kernel(core_ref, mine_ref, other_ref, weight_ref, triangle_ref, lower_ref, a_ref, x_ref, u_ref, y_ref, v_ref):
        full_row = lax.broadcasted_iota(jnp.int32, (size, size), 0)
        full_lane = lax.broadcasted_iota(jnp.int32, (size, size), 1)
        first = core_ref[0] == 0

        def whole(k):
            low = jnp.where(first, mine_ref[k], other_ref[k])
            high = jnp.where(first, other_ref[k], mine_ref[k])
            corner = jnp.concatenate([low[quarter:], high[quarter:]], 0)
            rows = jnp.concatenate([low[:quarter], high[:quarter], pltpu.roll(corner, half, 1), corner], 0)
            rows = rows * (1.0 / cells)
            return jnp.where(full_lane >= full_row, rows, rows.T)

        gram, extra = whole(0), whole(1)
        a_ref[...] = gram
        eliminate(a_ref, x_ref, u_ref)
        upper = u_ref[...]
        eye = jnp.where(full_row == full_lane, 1.0, 0.0)
        inverse = refined(x_ref[...], upper, eye)
        lower_ref[...] = upper.T
        rest = residual(gram, upper) + extra
        change = matmul(matmul(inverse, rest), inverse, ((1,), (1,)))
        change = jnp.where(full_lane <= full_row, change, change.T)
        small = jnp.sum(change * change) < 2.0**-12

        @pl.when(small)
        def _():
            keep = jnp.where(full_lane < full_row, 1.0, jnp.where(full_lane == full_row, 0.5, 0.0))
            step = keep * change
            for _ in range(3):
                step = keep * (change - matmul(step, step, ((1,), (1,))))
            weight = inverse
            for _ in range(4):
                weight = inverse - matmul(step, weight)
            weight_ref[...] = weight
            triangle_ref[...] = upper + matmul(step, upper, ((0,), (0,)))

        @pl.when(jnp.logical_not(small))
        def _():
            a_ref[...] = change + eye
            eliminate(a_ref, y_ref, v_ref)
            weight_ref[...] = matmul(refined(y_ref[...], v_ref[...], eye), inverse)
            triangle_ref[...] = matmul(v_ref[...], upper)

    square = jax.ShapeDtypeStruct((size, size), jnp.float32)
    vmem = pl.BlockSpec(memory_space=pltpu.VMEM)
    return pl.pallas_call(
        kernel,
        in_specs=[pl.BlockSpec(memory_space=pltpu.SMEM), vmem, vmem],
        out_specs=[vmem, vmem, vmem],
        out_shape=[square, square, square],
        scratch_shapes=[pltpu.VMEM((size, size), jnp.float32)] * 5,
        name="factor",
    )(core, mine, other)


def refined(inverse, upper, eye):
    return inverse + matmul(eye - matmul(inverse, upper, ((1,), (1,))), inverse)


def two_sum(left, right):
    total = left + right
    back = total - left
    return total, (left - (total - back)) + (right - back)


def gram_halves(parts, core, chunk=2048, piece=512):
    cells = parts[0].shape[1]
    count = len(parts)
    size = sum(part.shape[0] for part in parts)
    half, quarter = size // 2, size // 4
    steps = cells // chunk

    def kernel(core_ref, *refs):
        part_refs = refs[:count]
        keep_ref, send_ref, high_ref, low_ref, cross_ref = refs[count:]
        step = pl.program_id(0)

        @pl.when(step == 0)
        def _():
            high_ref[...] = jnp.zeros_like(high_ref)
            low_ref[...] = jnp.zeros_like(low_ref)
            cross_ref[...] = jnp.zeros_like(cross_ref)

        for k in range(chunk // piece):
            span = slice(k * piece, (k + 1) * piece)
            block = jnp.concatenate([ref[:, span] for ref in part_refs], 0)
            first, second, third, _ = split(block, jnp.max(jnp.abs(block), 1, keepdims=True))
            lhs = jnp.concatenate([first, second, third], 0).astype(jnp.bfloat16)
            part = lax.dot_general(
                lhs, lhs[: 2 * size], (((1,), (1,)), ((), ())), preferred_element_type=jnp.float32
            )
            high_ref[...], error = two_sum(high_ref[...], part[:size, :size])
            low_ref[...] += error + part[size : 2 * size, size:]
            cross_ref[...] += part[size : 2 * size, :size] + (part[2 * size :, :size] + part[2 * size :, size:])

        @pl.when(step == steps - 1)
        def _():
            cross = cross_ref[...]
            high_ref[...], low_ref[...] = two_sum(high_ref[...], low_ref[...] + (cross + cross.T))
            lane = lax.broadcasted_iota(jnp.int32, (quarter, size), 1)
            lead = core_ref[0] == 0
            for k, ref in enumerate((high_ref, low_ref)):
                corner = jnp.where(lane < half, pltpu.roll(ref[half : half + quarter, :], half, 1), ref[half + quarter :, :])
                low = jnp.concatenate([ref[:quarter, :], corner[: quarter // 2]], 0)
                high = jnp.concatenate([ref[quarter:half, :], corner[quarter // 2 :]], 0)
                keep_ref[k] = jnp.where(lead, low, high)
                send_ref[k] = jnp.where(lead, high, low)

    out = jax.ShapeDtypeStruct((2, quarter + quarter // 2, size), jnp.float32)
    spec = pl.BlockSpec((2, quarter + quarter // 2, size), lambda i: (0, 0, 0))
    return pl.pallas_call(
        kernel,
        grid=(steps,),
        in_specs=[
            pl.BlockSpec(memory_space=pltpu.SMEM),
            *[pl.BlockSpec((part.shape[0], chunk), lambda i: (0, i)) for part in parts],
        ],
        out_specs=[spec, spec],
        out_shape=[out, out],
        scratch_shapes=[pltpu.VMEM((size, size), jnp.float32)] * 3,
        name="gram_halves",
    )(core, *parts)


def apply_split(weight, parts, nx, nz, ny):
    count = sum(part.shape[0] for part in parts)
    halves = ny // LANES

    def kernel(w_ref, *refs):
        part_refs, out_ref = refs[:-1], refs[-1]
        w1, w2, w3 = three_parts(w_ref[...])
        lhs = jnp.concatenate(
            [
                jnp.concatenate([w1, w2], 1),
                jnp.concatenate([w2, w1], 1),
                jnp.concatenate([w3, jnp.zeros_like(w3)], 1),
            ],
            0,
        ).astype(jnp.bfloat16)
        block = jnp.concatenate([ref[...] for ref in part_refs], 0)
        s1, s2, s3 = three_parts(block)
        pair = jnp.concatenate([s1, s2], 0).astype(jnp.bfloat16)
        dims = (((1,), (0,)), ((), ()))
        main = lax.dot_general(lhs, pair, dims, preferred_element_type=jnp.float32)
        tail = lax.dot_general(w1.astype(jnp.bfloat16), s3.astype(jnp.bfloat16), dims, preferred_element_type=jnp.float32)
        result = main[:count] + (main[count : 2 * count] + (main[2 * count :] + tail))
        flat = out_ref.reshape(count * nz, LANES)
        for z in range(nz):
            flat[pl.ds(z, count, stride=nz), :] = result[:, z * LANES : (z + 1) * LANES]

    return pl.pallas_call(
        kernel,
        grid=(nx, halves),
        in_specs=[
            pl.BlockSpec((count, count), lambda i, h: (0, 0)),
            *[pl.BlockSpec((part.shape[0], nz * LANES), lambda i, h: (0, i * halves + h)) for part in parts],
        ],
        out_specs=pl.BlockSpec((count, 1, nz, LANES), lambda i, h: (0, i, 0, h)),
        out_shape=jax.ShapeDtypeStruct((count, nx, nz, ny), jnp.float32),
        name="apply_split",
    )(weight, *parts)


def shifted(value, axis, forward):
    count = lax.axis_size(axis)
    step = 1 if forward else count - 1
    return lax.ppermute(value, axis, [(i, (i + step) % count) for i in range(count)])


def flipped(value, flip_x, flip_z):
    size_x, size_z = lax.axis_size("gx"), lax.axis_size("gz")
    pairs = [
        (x * size_z + z, (x ^ flip_x) * size_z + (z ^ flip_z)) for x in range(size_x) for z in range(size_z)
    ]
    return lax.ppermute(value, ("gx", "gz"), pairs)


def pair_sum(left, right):
    high, error = two_sum(left[0], right[0])
    return jnp.stack([high, left[1] + right[1] + error])


def all_sum(keep, send):
    value = pair_sum(keep, flipped(send, 1, 0))
    flips = [(2, 0), (6, 0), (8, 0), (24, 0), (0, 1), (0, 2), (0, 6)]
    for flip_x, flip_z in flips:
        value = pair_sum(value, flipped(value, flip_x, flip_z))
    return value, flipped(value, 1, 0)


def shards(velocity, scaled_modes):
    _, _, cells_x, cells_z, cells_y = velocity.shape
    total_cells = cells_x * lax.axis_size("gx") * cells_z * lax.axis_size("gz") * cells_y
    core = (lax.axis_index("gx") % 2).astype(jnp.int32).reshape(1)
    halos = []
    for begin, count in SPANS:
        first_x, last_x, first_z, last_z = pack_faces(velocity, begin, count)
        low_x, high_x = shifted(last_x, "gx", True), shifted(first_x, "gx", False)
        low_z, high_z = shifted(last_z, "gz", True), shifted(first_z, "gz", False)
        halos.append((low_x, high_x, low_z, high_z))
    parts = [flatten_modes(scaled_modes)]
    for (begin, _), halo in zip(SPANS, halos):
        parts.append(criterion(velocity, *halo, begin))
    mine, other = all_sum(*gram_halves(parts, core))
    weight, triangle, lower_one = factor(mine, other, core, float(total_cells))
    basis = apply_split(weight, parts, cells_x, cells_z, cells_y)
    return basis, triangle, lower_one


def solution(mesh):
    in_specs = (P(None, None, "gx", "gz", None), P(None, "gx", "gz", None))
    out_specs = (P(None, "gx", "gz", None), P(), P())
    return jax.shard_map(shards, mesh=mesh, in_specs=in_specs, out_specs=out_specs, check_vma=False)
```

```python
import jax
import jax.numpy as jnp
from jax import lax
from jax.experimental import pallas as pl
from jax.experimental.pallas import tpu as pltpu
from jax.sharding import PartitionSpec as P


precise = lax.Precision.HIGHEST
coarse = lax.Precision.DEFAULT
LANES = 128
GRANT = 59 * 2**20
SPANS = ((0, 32), (32, 32))


def pack_faces(velocity, begin, snaps, group=16):
    _, comps, nx, nz, ny = velocity.shape
    skip = begin // group
    halves = ny // LANES
    rows = group * comps * nx

    def kernel(*refs):
        views, (first_x, last_x, first_z, last_z) = refs[:halves], refs[halves:]
        for h, v_ref in enumerate(views):
            lanes = slice(h * LANES, (h + 1) * LANES)
            first_x[:, :, :, lanes] = v_ref[:, :, 0]
            last_x[:, :, :, lanes] = v_ref[:, :, nx - 1]
            flat = v_ref.reshape(rows * nz, LANES)
            first_z[h] = flat[pl.ds(0, rows, stride=nz), :]
            last_z[h] = flat[pl.ds(nz - 1, rows, stride=nz), :]

    face_x = jax.ShapeDtypeStruct((snaps, comps, nz, ny), velocity.dtype)
    face_z = jax.ShapeDtypeStruct((halves, snaps * comps * nx, LANES), velocity.dtype)
    spec_x = pl.BlockSpec((group, comps, nz, ny), lambda i: (i, 0, 0, 0))
    spec_z = pl.BlockSpec((halves, rows, LANES), lambda i: (0, i, 0))
    block = (group, comps, nx, nz, LANES)
    return pl.pallas_call(
        kernel,
        grid=(snaps // group,),
        in_specs=[pl.BlockSpec(block, lambda i, h=h: (i + skip, 0, 0, 0, h)) for h in range(halves)],
        out_specs=[spec_x, spec_x, spec_z, spec_z],
        out_shape=[face_x, face_x, face_z, face_z],
        compiler_params=pltpu.CompilerParams(vmem_limit_bytes=GRANT),
        name="pack_faces",
    )(*[velocity] * halves)


def flatten_modes(modes, group=2):
    count, nx, nz, ny = modes.shape
    halves = ny // LANES

    def kernel(*refs):
        out_ref = refs[halves]
        for h in range(halves):
            flat = refs[h].reshape(count * group * nz, LANES)
            for x in range(group):
                for z in range(nz):
                    start = ((x * halves + h) * nz + z) * LANES
                    out_ref[:, start : start + LANES] = flat[pl.ds(x * nz + z, count, stride=group * nz), :]

    block = (count, group, nz, LANES)
    return pl.pallas_call(
        kernel,
        grid=(nx // group,),
        in_specs=[pl.BlockSpec(block, lambda i, h=h: (0, i, 0, h)) for h in range(halves)],
        out_specs=pl.BlockSpec((count, group * nz * ny), lambda i: (0, i)),
        out_shape=jax.ShapeDtypeStruct((count, nx * nz * ny), modes.dtype),
        compiler_params=pltpu.CompilerParams(vmem_limit_bytes=GRANT),
        name="flatten_modes",
    )(*[modes] * halves)


def criterion(velocity, low_x, high_x, low_z, high_z, begin, group=8):
    _, comps, nx, nz, ny = velocity.shape
    snaps = low_x.shape[0]
    skip = begin // group
    halves = ny // LANES

    def kernel(v_ref, lx_ref, hx_ref, lz_ref, hz_ref, out_ref, q_ref):
        lane = lax.broadcasted_iota(jnp.int32, (nz, LANES), 1)
        level = lax.broadcasted_iota(jnp.int32, (nz, LANES), 0)

        def cut(half):
            return slice(half * LANES, (half + 1) * LANES)

        def wall(parts):
            below = [pltpu.roll(p, 1, 1) for p in parts]
            above = [pltpu.roll(p, LANES - 1, 1) for p in parts]
            out = []
            for h in range(halves):
                here = parts[h]
                fp = jnp.where(lane == LANES - 1, above[h + 1], above[h]) if h < halves - 1 else above[h]
                if h:
                    fm = jnp.where(lane == 0, below[h - 1], below[h])
                else:
                    edge = 3.0 * (here - fp) + pltpu.roll(here, LANES - 2, 1)
                    fm = jnp.where(lane == 0, edge, below[h])
                if h == halves - 1:
                    edge = 3.0 * (here - fm) + pltpu.roll(here, 2, 1)
                    fp = jnp.where(lane == LANES - 1, edge, fp)
                d = fp - fm
                out.append(d)
            return out

        def body(s, carry):
            t = pl.program_id(0) * group + s
            for x in range(nx):
                dx, dz, dy = [], [], []
                for c in range(comps):
                    here = [v_ref[s, c, x, :, cut(h)] for h in range(halves)]
                    dx.append([
                        (v_ref[s, c, x + 1, :, cut(h)] if x < nx - 1 else hx_ref[t, c, :, cut(h)])
                        - (v_ref[s, c, x - 1, :, cut(h)] if x else lx_ref[t, c, :, cut(h)])
                        for h in range(halves)
                    ])
                    row = (t * comps + c) * nx + x
                    part = []
                    for h in range(halves):
                        up = jnp.where(level == nz - 1, hz_ref.at[h][pl.ds(row, nz, stride=0), :], pltpu.roll(here[h], nz - 1, 0))
                        down = jnp.where(level == 0, lz_ref.at[h][pl.ds(row, nz, stride=0), :], pltpu.roll(here[h], 1, 0))
                        part.append(up - down)
                    dz.append(part)
                    dy.append(wall(here))
                for h in range(halves):
                    diagonal = dx[0][h] * dx[0][h] + dz[1][h] * dz[1][h] + dy[2][h] * dy[2][h]
                    cross = dz[0][h] * dx[1][h] + dy[0][h] * dx[2][h] + dy[1][h] * dz[2][h]
                    q_ref[h, pl.ds((s * nx + x) * nz, nz), :] = -0.125 * diagonal - 0.25 * cross
            return carry

        lax.fori_loop(0, group, body, 0, unroll=4)
        for x in range(nx):
            for z in range(nz):
                for h in range(halves):
                    start = ((x * halves + h) * nz + z) * LANES
                    view = q_ref.at[h]
                    out_ref[:, start : start + LANES] = view[pl.ds(x * nz + z, group, stride=nx * nz), :]

    near = pl.BlockSpec(memory_space=pltpu.VMEM)
    return pl.pallas_call(
        kernel,
        grid=(snaps // group,),
        in_specs=[pl.BlockSpec((group, comps, nx, nz, ny), lambda i: (i + skip, 0, 0, 0, 0)), near, near, near, near],
        out_specs=pl.BlockSpec((group, nx * nz * ny), lambda i: (i, 0)),
        out_shape=jax.ShapeDtypeStruct((snaps, nx * nz * ny), velocity.dtype),
        scratch_shapes=[pltpu.VMEM((halves, group * nx * nz, LANES), velocity.dtype)],
        compiler_params=pltpu.CompilerParams(vmem_limit_bytes=GRANT),
        name="criterion",
    )(velocity, *[pltpu.with_memory_space_constraint(halo, pltpu.VMEM) for halo in (low_x, high_x, low_z, high_z)])


def spread(row, shape):
    return jnp.broadcast_to(row, shape)


def three_parts(value):
    first = value.astype(jnp.bfloat16).astype(jnp.float32)
    rest = value - first
    second = rest.astype(jnp.bfloat16).astype(jnp.float32)
    return first, second, rest - second


def eliminate(a_ref, x_ref, u_ref):
    size = a_ref.shape[0]
    tall = 8
    row = lax.broadcasted_iota(jnp.int32, (tall, size), 0)
    lane = lax.broadcasted_iota(jnp.int32, (tall, size), 1)
    full = (tall, size)
    full_row = lax.broadcasted_iota(jnp.int32, (size, size), 0)
    full_lane = lax.broadcasted_iota(jnp.int32, (size, size), 1)
    x_ref[...] = jnp.where(full_row == full_lane, 1.0, 0.0)
    for start in range(0, size, tall):
        rows = slice(start, start + tall)
        left, right = a_ref[rows, :], x_ref[rows, :]
        columns = [spread(left[:, start + j : start + j + 1], full) for j in range(tall)]
        pivots = jnp.ones(full, jnp.float32)
        for j in range(tall):
            pivot = spread(columns[j][j : j + 1, :], full)
            pivots = jnp.where(row == j, pivot, pivots)
            if j == tall - 1:
                break
            factor = jnp.where(row > j, columns[j] * (1.0 / pivot), 0.0)
            for k in range(j + 1, tall):
                columns[k] = columns[k] - factor * spread(columns[k][j : j + 1, :], full)
            left = left - factor * spread(left[j : j + 1, :], full)
            right = right - factor * spread(right[j : j + 1, :], full)
        scale = 1.0 / jnp.sqrt(pivots)
        left = jnp.where(lane >= start + row, left * scale, 0.0)
        right = right * scale
        u_ref[rows, :] = left
        x_ref[rows, :] = right
        if start + tall < size:
            l1, l2, l3 = three_parts(left)
            r1, r2, r3 = three_parts(right)
            lhs = jnp.concatenate([l1, l1, l2, l2, l1, l3], 0).astype(jnp.bfloat16)
            rhs_left = jnp.concatenate([l1, l2, l1, l2, l3, l1], 0).astype(jnp.bfloat16)
            rhs_right = jnp.concatenate([r1, r2, r1, r2, r3, r1], 0).astype(jnp.bfloat16)
            rhs = jnp.concatenate([rhs_left, rhs_right], 1)
            change = lax.dot_general(lhs, rhs, (((0,), (0,)), ((), ())), preferred_element_type=jnp.float32)
            below = slice(start + tall, size)
            a_ref[below, :] -= change[start + tall :, :size]
            x_ref[below, :] -= change[start + tall :, size:]


def matmul(left, right, dims=((1,), (0,)), precision=precise):
    return lax.dot_general(left, right, (dims, ((), ())), precision=precision, preferred_element_type=jnp.float32)


def split(value, top):
    big = top * (1.5 * 2.0**16)
    first = (value + big) - big
    rest = value - first
    second = rest.astype(jnp.bfloat16).astype(jnp.float32)
    rest = rest - second
    third = rest.astype(jnp.bfloat16).astype(jnp.float32)
    return first, second, third, rest - third


def residual(gram, upper):
    parts = [p.astype(jnp.bfloat16) for p in split(upper, jnp.max(jnp.abs(upper), 0, keepdims=True))]

    def cross(i, j):
        return lax.dot_general(parts[i], parts[j], (((0,), (0,)), ((), ())), preferred_element_type=jnp.float32)

    out = gram - cross(0, 0)
    both = cross(1, 0)
    out = out - (both + both.T)
    both = cross(2, 0) + (cross(3, 0) + cross(2, 1))
    return out - (cross(1, 1) + (both + both.T))


def factor(mine, other, core, cells):
    size = mine.shape[2]
    half = size // 2
    quarter = half // 2

    def kernel(core_ref, mine_ref, other_ref, weight_ref, triangle_ref, lower_ref, a_ref, x_ref, u_ref, y_ref, v_ref):
        full_row = lax.broadcasted_iota(jnp.int32, (size, size), 0)
        full_lane = lax.broadcasted_iota(jnp.int32, (size, size), 1)
        first = core_ref[0] == 0

        def whole(k):
            low = jnp.where(first, mine_ref[k], other_ref[k])
            high = jnp.where(first, other_ref[k], mine_ref[k])
            base = jnp.concatenate([low[:quarter], high[:quarter]], 0) * (1.0 / cells)
            diagonal = jnp.broadcast_to(low[quarter : quarter + 1] * (1.0 / cells), (size, size))
            rows = jnp.concatenate([base, pltpu.roll(base, half, 1)], 0)
            late = full_row >= half
            inside = jnp.logical_and(full_lane >= half, full_lane < full_row)
            own = jnp.logical_or(
                jnp.logical_and(jnp.logical_not(late), full_lane >= full_row), jnp.logical_and(late, inside)
            )
            rows = jnp.where(own, rows, rows.T)
            return jnp.where(jnp.logical_and(late, full_lane == full_row), diagonal, rows)

        gram, extra = whole(0), whole(1)
        a_ref[...] = gram
        eliminate(a_ref, x_ref, u_ref)
        upper = u_ref[...]
        eye = jnp.where(full_row == full_lane, 1.0, 0.0)
        inverse = refined(x_ref[...], upper, eye)
        lower_ref[...] = upper.T
        rest = residual(gram, upper) + extra
        change = matmul(matmul(inverse, rest), inverse, ((1,), (1,)))
        change = jnp.where(full_lane <= full_row, change, change.T)
        small = jnp.sum(change * change) < 2.0**-12

        @pl.when(small)
        def _():
            keep = jnp.where(full_lane < full_row, 1.0, jnp.where(full_lane == full_row, 0.5, 0.0))
            step = keep * change
            for precision in (coarse, coarse, precise):
                step = keep * (change - matmul(step, step, ((1,), (1,)), precision))
            weight = inverse
            for precision in (coarse, coarse, precise, precise):
                weight = inverse - matmul(step, weight, precision=precision)
            weight_ref[...] = weight
            triangle_ref[...] = upper + matmul(step, upper, ((0,), (0,)))

        @pl.when(jnp.logical_not(small))
        def _():
            a_ref[...] = change + eye
            eliminate(a_ref, y_ref, v_ref)
            weight_ref[...] = matmul(refined(y_ref[...], v_ref[...], eye), inverse)
            triangle_ref[...] = matmul(v_ref[...], upper)

    square = jax.ShapeDtypeStruct((size, size), jnp.float32)
    vmem = pl.BlockSpec(memory_space=pltpu.VMEM)
    return pl.pallas_call(
        kernel,
        in_specs=[pl.BlockSpec(memory_space=pltpu.SMEM), vmem, vmem],
        out_specs=[vmem, vmem, vmem],
        out_shape=[square, square, square],
        scratch_shapes=[pltpu.VMEM((size, size), jnp.float32)] * 5,
        name="factor",
    )(core, *[pltpu.with_memory_space_constraint(value, pltpu.VMEM) for value in (mine, other)])


def refined(inverse, upper, eye):
    return inverse + matmul(eye - matmul(inverse, upper, ((1,), (1,))), inverse)


def two_sum(left, right):
    total = left + right
    back = total - left
    return total, (left - (total - back)) + (right - back)


def gram_halves(parts, core, chunk=2048, piece=512):
    cells = parts[0].shape[1]
    count = len(parts)
    size = sum(part.shape[0] for part in parts)
    half, quarter = size // 2, size // 4
    steps = cells // chunk

    def kernel(core_ref, *refs):
        part_refs = refs[:count]
        keep_ref, send_ref, high_ref, low_ref, cross_ref = refs[count:]
        step = pl.program_id(0)

        @pl.when(step == 0)
        def _():
            high_ref[...] = jnp.zeros_like(high_ref)
            low_ref[...] = jnp.zeros_like(low_ref)
            cross_ref[...] = jnp.zeros_like(cross_ref)

        for k in range(chunk // piece):
            span = slice(k * piece, (k + 1) * piece)
            block = jnp.concatenate([ref[:, span] for ref in part_refs], 0)
            first, second, third, _ = split(block, jnp.max(jnp.abs(block), 1, keepdims=True))
            lhs = jnp.concatenate([first, second, third], 0).astype(jnp.bfloat16)
            part = lax.dot_general(
                lhs, lhs[: 2 * size], (((1,), (1,)), ((), ())), preferred_element_type=jnp.float32
            )
            high_ref[...], error = two_sum(high_ref[...], part[:size, :size])
            low_ref[...] += error + part[size : 2 * size, size:]
            cross_ref[...] += part[size : 2 * size, :size] + (part[2 * size :, :size] + part[2 * size :, size:])

        @pl.when(step == steps - 1)
        def _():
            cross = cross_ref[...]
            high_ref[...], low_ref[...] = two_sum(high_ref[...], low_ref[...] + (cross + cross.T))
            lane = lax.broadcasted_iota(jnp.int32, (half, size), 1)
            row = lax.broadcasted_iota(jnp.int32, (half, size), 0)
            lead = core_ref[0] == 0
            for k, ref in enumerate((high_ref, low_ref)):
                corner = ref[half:, :]
                base = jnp.where(lane < row, pltpu.roll(corner, half, 1), ref[:half, :])
                diagonal = jnp.sum(jnp.where(lane == row + half, corner, 0.0), 0, keepdims=True)
                extra = jnp.broadcast_to(diagonal, (8, size))
                low = jnp.concatenate([base[:quarter], extra], 0)
                high = jnp.concatenate([base[quarter:], extra], 0)
                keep_ref[k] = jnp.where(lead, low, high)
                send_ref[k] = jnp.where(lead, high, low)

    out = jax.ShapeDtypeStruct((2, quarter + 8, size), jnp.float32)
    spec = pl.BlockSpec((2, quarter + 8, size), lambda i: (0, 0, 0))
    return pl.pallas_call(
        kernel,
        grid=(steps,),
        in_specs=[
            pl.BlockSpec(memory_space=pltpu.SMEM),
            *[pl.BlockSpec((part.shape[0], chunk), lambda i: (0, i)) for part in parts],
        ],
        out_specs=[spec, spec],
        out_shape=[out, out],
        scratch_shapes=[pltpu.VMEM((size, size), jnp.float32)] * 3,
        name="gram_halves",
    )(core, *parts)


def apply_split(weight, parts, nx, nz, ny):
    count = sum(part.shape[0] for part in parts)
    halves = ny // LANES

    def kernel(w_ref, *refs):
        part_refs, out_ref = refs[:-1], refs[-1]
        w1, w2, w3 = three_parts(w_ref[...])
        lhs = jnp.concatenate(
            [
                jnp.concatenate([w1, w2], 1),
                jnp.concatenate([w2, w1], 1),
                jnp.concatenate([w3, jnp.zeros_like(w3)], 1),
            ],
            0,
        ).astype(jnp.bfloat16)
        block = jnp.concatenate([ref[...] for ref in part_refs], 0)
        s1, s2, s3 = three_parts(block)
        pair = jnp.concatenate([s1, s2], 0).astype(jnp.bfloat16)
        dims = (((1,), (0,)), ((), ()))
        main = lax.dot_general(lhs, pair, dims, preferred_element_type=jnp.float32)
        tail = lax.dot_general(w1.astype(jnp.bfloat16), s3.astype(jnp.bfloat16), dims, preferred_element_type=jnp.float32)
        result = main[:count] + (main[count : 2 * count] + (main[2 * count :] + tail))
        flat = out_ref.reshape(count * nz, LANES)
        for z in range(nz):
            flat[pl.ds(z, count, stride=nz), :] = result[:, z * LANES : (z + 1) * LANES]

    return pl.pallas_call(
        kernel,
        grid=(nx, halves),
        in_specs=[
            pl.BlockSpec((count, count), lambda i, h: (0, 0)),
            *[pl.BlockSpec((part.shape[0], nz * LANES), lambda i, h: (0, i * halves + h)) for part in parts],
        ],
        out_specs=pl.BlockSpec((count, 1, nz, LANES), lambda i, h: (0, i, 0, h)),
        out_shape=jax.ShapeDtypeStruct((count, nx, nz, ny), jnp.float32),
        name="apply_split",
    )(weight, *parts)


def shifted(value, axis, forward):
    count = lax.axis_size(axis)
    step = 1 if forward else count - 1
    return lax.ppermute(value, axis, [(i, (i + step) % count) for i in range(count)])


def flipped(value, flip_x, flip_z):
    size_x, size_z = lax.axis_size("gx"), lax.axis_size("gz")
    pairs = [
        (x * size_z + z, (x ^ flip_x) * size_z + (z ^ flip_z)) for x in range(size_x) for z in range(size_z)
    ]
    return lax.ppermute(value, ("gx", "gz"), pairs)


def pair_sum(left, right):
    high, error = two_sum(left[0], right[0])
    return jnp.stack([high, left[1] + right[1] + error])


def all_sum(keep, send):
    value = pair_sum(keep, flipped(send, 1, 0))
    flips = [(2, 0), (6, 0), (8, 0), (24, 0), (0, 1), (0, 2), (0, 6)]
    for flip_x, flip_z in flips:
        value = pair_sum(value, flipped(value, flip_x, flip_z))
    return value, flipped(value, 1, 0)


def shards(velocity, scaled_modes):
    _, _, cells_x, cells_z, cells_y = velocity.shape
    total_cells = cells_x * lax.axis_size("gx") * cells_z * lax.axis_size("gz") * cells_y
    core = (lax.axis_index("gx") % 2).astype(jnp.int32).reshape(1)
    halos = []
    for begin, count in SPANS:
        first_x, last_x, first_z, last_z = pack_faces(velocity, begin, count)
        low_x = shifted(last_x, "gx", True)
        high_x = shifted(first_x, "gx", False)
        low_z = shifted(last_z, "gz", True)
        high_z = shifted(first_z, "gz", False)
        halos.append((low_x, high_x, low_z, high_z))
    parts = [flatten_modes(scaled_modes)]
    for (begin, _), halo in zip(SPANS, halos):
        parts.append(criterion(velocity, *halo, begin))
    mine, other = all_sum(*gram_halves(parts, core))
    weight, triangle, lower_one = factor(mine, other, core, float(total_cells))
    basis = apply_split(weight, parts, cells_x, cells_z, cells_y)
    return basis, triangle, lower_one


def solution(mesh):
    in_specs = (P(None, None, "gx", "gz", None), P(None, "gx", "gz", None))
    out_specs = (P(None, "gx", "gz", None), P(), P())
    return jax.shard_map(shards, mesh=mesh, in_specs=in_specs, out_specs=out_specs, check_vma=False)
```

```python
import jax
import jax.numpy as jnp
from jax import lax
from jax.experimental import pallas as pl
from jax.experimental.pallas import tpu as pltpu
from jax.sharding import PartitionSpec as P


precise = lax.Precision.HIGHEST
coarse = lax.Precision.DEFAULT
LANES = 128
GRANT = 57 * 2**20
SPANS = ((0, 32), (32, 32))


def pack_faces(velocity, begin, snaps, group=16):
    _, comps, nx, nz, ny = velocity.shape
    skip = begin // group
    halves = ny // LANES
    rows = group * comps * nx

    def kernel(*refs):
        views, (first_x, last_x, first_z, last_z) = refs[:halves], refs[halves:]
        for h, v_ref in enumerate(views):
            lanes = slice(h * LANES, (h + 1) * LANES)
            first_x[:, :, :, lanes] = v_ref[:, :, 0]
            last_x[:, :, :, lanes] = v_ref[:, :, nx - 1]
            flat = v_ref.reshape(rows * nz, LANES)
            first_z[h] = flat[pl.ds(0, rows, stride=nz), :]
            last_z[h] = flat[pl.ds(nz - 1, rows, stride=nz), :]

    face_x = jax.ShapeDtypeStruct((snaps, comps, nz, ny), velocity.dtype)
    face_z = jax.ShapeDtypeStruct((halves, snaps * comps * nx, LANES), velocity.dtype)
    spec_x = pl.BlockSpec((group, comps, nz, ny), lambda i: (i, 0, 0, 0))
    spec_z = pl.BlockSpec((halves, rows, LANES), lambda i: (0, i, 0))
    block = (group, comps, nx, nz, LANES)
    return pl.pallas_call(
        kernel,
        grid=(snaps // group,),
        in_specs=[pl.BlockSpec(block, lambda i, h=h: (i + skip, 0, 0, 0, h)) for h in range(halves)],
        out_specs=[spec_x, spec_x, spec_z, spec_z],
        out_shape=[face_x, face_x, face_z, face_z],
        compiler_params=pltpu.CompilerParams(vmem_limit_bytes=GRANT),
        name="pack_faces",
    )(*[velocity] * halves)


def flatten_modes(modes, group=2):
    count, nx, nz, ny = modes.shape
    halves = ny // LANES

    def kernel(*refs):
        out_ref = refs[halves]
        for h in range(halves):
            flat = refs[h].reshape(count * group * nz, LANES)
            for x in range(group):
                for z in range(nz):
                    start = ((x * halves + h) * nz + z) * LANES
                    out_ref[:, start : start + LANES] = flat[pl.ds(x * nz + z, count, stride=group * nz), :]

    block = (count, group, nz, LANES)
    return pl.pallas_call(
        kernel,
        grid=(nx // group,),
        in_specs=[pl.BlockSpec(block, lambda i, h=h: (0, i, 0, h)) for h in range(halves)],
        out_specs=pl.BlockSpec((count, group * nz * ny), lambda i: (0, i)),
        out_shape=jax.ShapeDtypeStruct((count, nx * nz * ny), modes.dtype),
        compiler_params=pltpu.CompilerParams(vmem_limit_bytes=GRANT),
        name="flatten_modes",
    )(*[modes] * halves)


def criterion(velocity, low_x, high_x, low_z, high_z, begin, group=8):
    _, comps, nx, nz, ny = velocity.shape
    snaps = low_x.shape[0]
    skip = begin // group
    halves = ny // LANES

    def kernel(v_ref, lx_ref, hx_ref, lz_ref, hz_ref, out_ref):
        flat = out_ref.reshape(nx * halves * nz * group, LANES)
        lane = lax.broadcasted_iota(jnp.int32, (nz, LANES), 1)
        level = lax.broadcasted_iota(jnp.int32, (nz, LANES), 0)

        def cut(half):
            return slice(half * LANES, (half + 1) * LANES)

        def wall(parts):
            below = [pltpu.roll(p, 1, 1) for p in parts]
            above = [pltpu.roll(p, LANES - 1, 1) for p in parts]
            out = []
            for h in range(halves):
                here = parts[h]
                fp = jnp.where(lane == LANES - 1, above[h + 1], above[h]) if h < halves - 1 else above[h]
                if h:
                    fm = jnp.where(lane == 0, below[h - 1], below[h])
                else:
                    edge = 3.0 * (here - fp) + pltpu.roll(here, LANES - 2, 1)
                    fm = jnp.where(lane == 0, edge, below[h])
                if h == halves - 1:
                    edge = 3.0 * (here - fm) + pltpu.roll(here, 2, 1)
                    fp = jnp.where(lane == LANES - 1, edge, fp)
                d = fp - fm
                out.append(d)
            return out

        def body(s, carry):
            t = pl.program_id(0) * group + s
            for x in range(nx):
                dx, dz, dy = [], [], []
                for c in range(comps):
                    here = [v_ref[s, c, x, :, cut(h)] for h in range(halves)]
                    dx.append([
                        (v_ref[s, c, x + 1, :, cut(h)] if x < nx - 1 else hx_ref[t, c, :, cut(h)])
                        - (v_ref[s, c, x - 1, :, cut(h)] if x else lx_ref[t, c, :, cut(h)])
                        for h in range(halves)
                    ])
                    row = (t * comps + c) * nx + x
                    part = []
                    for h in range(halves):
                        up = jnp.where(level == nz - 1, hz_ref.at[h][pl.ds(row, nz, stride=0), :], pltpu.roll(here[h], nz - 1, 0))
                        down = jnp.where(level == 0, lz_ref.at[h][pl.ds(row, nz, stride=0), :], pltpu.roll(here[h], 1, 0))
                        part.append(up - down)
                    dz.append(part)
                    dy.append(wall(here))
                for h in range(halves):
                    diagonal = dx[0][h] * dx[0][h] + dz[1][h] * dz[1][h] + dy[2][h] * dy[2][h]
                    cross = dz[0][h] * dx[1][h] + dy[0][h] * dx[2][h] + dy[1][h] * dz[2][h]
                    flat[pl.ds((x * halves + h) * nz * group + s, nz, stride=group), :] = -0.125 * diagonal - 0.25 * cross
            return carry

        lax.fori_loop(0, group, body, 0, unroll=4)

    near = pl.BlockSpec(memory_space=pltpu.VMEM)
    return pl.pallas_call(
        kernel,
        grid=(snaps // group,),
        in_specs=[pl.BlockSpec((group, comps, nx, nz, ny), lambda i: (i + skip, 0, 0, 0, 0)), near, near, near, near],
        out_specs=pl.BlockSpec((1, nx * halves * nz, group, LANES), lambda i: (i, 0, 0, 0)),
        out_shape=jax.ShapeDtypeStruct((snaps // group, nx * halves * nz, group, LANES), velocity.dtype),
        compiler_params=pltpu.CompilerParams(vmem_limit_bytes=GRANT),
        name="criterion",
    )(velocity, *[pltpu.with_memory_space_constraint(halo, pltpu.VMEM) for halo in (low_x, high_x, low_z, high_z)])


def columns(ref, begin, count):
    if len(ref.shape) == 2:
        return ref[:, begin * LANES : (begin + count) * LANES]
    return jnp.concatenate([ref[:, t].reshape(-1, LANES) for t in range(begin, begin + count)], 1)


def rows_of(part):
    return part.shape[0] if len(part.shape) == 2 else part.shape[0] * part.shape[2]


def window(part, count, index):
    if len(part.shape) == 2:
        return pl.BlockSpec((part.shape[0], count * LANES), lambda *ids: (0, index(*ids)))
    return pl.BlockSpec((part.shape[0], count, part.shape[2], LANES), lambda *ids: (0, index(*ids), 0, 0))


def spread(row, shape):
    return jnp.broadcast_to(row, shape)


def three_parts(value):
    first = value.astype(jnp.bfloat16).astype(jnp.float32)
    rest = value - first
    second = rest.astype(jnp.bfloat16).astype(jnp.float32)
    return first, second, rest - second


def eliminate(a_ref, x_ref, u_ref):
    size = a_ref.shape[0]
    tall = 8
    row = lax.broadcasted_iota(jnp.int32, (tall, size), 0)
    lane = lax.broadcasted_iota(jnp.int32, (tall, size), 1)
    full = (tall, size)
    full_row = lax.broadcasted_iota(jnp.int32, (size, size), 0)
    full_lane = lax.broadcasted_iota(jnp.int32, (size, size), 1)
    x_ref[...] = jnp.where(full_row == full_lane, 1.0, 0.0)
    for start in range(0, size, tall):
        rows = slice(start, start + tall)
        left, right = a_ref[rows, :], x_ref[rows, :]
        columns = [spread(left[:, start + j : start + j + 1], full) for j in range(tall)]
        pivots = jnp.ones(full, jnp.float32)
        for j in range(tall):
            pivot = spread(columns[j][j : j + 1, :], full)
            pivots = jnp.where(row == j, pivot, pivots)
            if j == tall - 1:
                break
            factor = jnp.where(row > j, columns[j] * (1.0 / pivot), 0.0)
            for k in range(j + 1, tall):
                columns[k] = columns[k] - factor * spread(columns[k][j : j + 1, :], full)
            left = left - factor * spread(left[j : j + 1, :], full)
            right = right - factor * spread(right[j : j + 1, :], full)
        scale = 1.0 / jnp.sqrt(pivots)
        left = jnp.where(lane >= start + row, left * scale, 0.0)
        right = right * scale
        u_ref[rows, :] = left
        x_ref[rows, :] = right
        if start + tall < size:
            l1, l2, l3 = three_parts(left)
            r1, r2, r3 = three_parts(right)
            lhs = jnp.concatenate([l1, l1, l2, l2, l1, l3], 0).astype(jnp.bfloat16)
            rhs_left = jnp.concatenate([l1, l2, l1, l2, l3, l1], 0).astype(jnp.bfloat16)
            rhs_right = jnp.concatenate([r1, r2, r1, r2, r3, r1], 0).astype(jnp.bfloat16)
            rhs = jnp.concatenate([rhs_left, rhs_right], 1)
            change = lax.dot_general(lhs, rhs, (((0,), (0,)), ((), ())), preferred_element_type=jnp.float32)
            below = slice(start + tall, size)
            a_ref[below, :] -= change[start + tall :, :size]
            x_ref[below, :] -= change[start + tall :, size:]


def matmul(left, right, dims=((1,), (0,)), precision=precise):
    return lax.dot_general(left, right, (dims, ((), ())), precision=precision, preferred_element_type=jnp.float32)


def split(value, top):
    big = top * (1.5 * 2.0**16)
    first = (value + big) - big
    rest = value - first
    second = rest.astype(jnp.bfloat16).astype(jnp.float32)
    rest = rest - second
    third = rest.astype(jnp.bfloat16).astype(jnp.float32)
    return first, second, third, rest - third


def residual(gram, upper):
    parts = [p.astype(jnp.bfloat16) for p in split(upper, jnp.max(jnp.abs(upper), 0, keepdims=True))]

    def cross(i, j):
        return lax.dot_general(parts[i], parts[j], (((0,), (0,)), ((), ())), preferred_element_type=jnp.float32)

    out = gram - cross(0, 0)
    both = cross(1, 0)
    out = out - (both + both.T)
    both = cross(2, 0) + (cross(3, 0) + cross(2, 1))
    return out - (cross(1, 1) + (both + both.T))


def factor(mine, other, core, cells):
    size = mine.shape[2]
    half = size // 2
    quarter = half // 2

    def kernel(core_ref, mine_ref, other_ref, weight_ref, triangle_ref, lower_ref, a_ref, x_ref, u_ref, y_ref, v_ref):
        full_row = lax.broadcasted_iota(jnp.int32, (size, size), 0)
        full_lane = lax.broadcasted_iota(jnp.int32, (size, size), 1)
        first = core_ref[0] == 0

        def whole(k):
            low = jnp.where(first, mine_ref[k], other_ref[k])
            high = jnp.where(first, other_ref[k], mine_ref[k])
            base = jnp.concatenate([low[:quarter], high[:quarter]], 0) * (1.0 / cells)
            diagonal = jnp.broadcast_to(low[quarter : quarter + 1] * (1.0 / cells), (size, size))
            rows = jnp.concatenate([base, pltpu.roll(base, half, 1)], 0)
            late = full_row >= half
            inside = jnp.logical_and(full_lane >= half, full_lane < full_row)
            own = jnp.logical_or(
                jnp.logical_and(jnp.logical_not(late), full_lane >= full_row), jnp.logical_and(late, inside)
            )
            rows = jnp.where(own, rows, rows.T)
            return jnp.where(jnp.logical_and(late, full_lane == full_row), diagonal, rows)

        gram, extra = whole(0), whole(1)
        a_ref[...] = gram
        eliminate(a_ref, x_ref, u_ref)
        upper = u_ref[...]
        eye = jnp.where(full_row == full_lane, 1.0, 0.0)
        inverse = refined(x_ref[...], upper, eye)
        lower_ref[...] = upper.T
        rest = residual(gram, upper) + extra
        change = matmul(matmul(inverse, rest), inverse, ((1,), (1,)))
        change = jnp.where(full_lane <= full_row, change, change.T)
        small = jnp.sum(change * change) < 2.0**-12

        @pl.when(small)
        def _():
            keep = jnp.where(full_lane < full_row, 1.0, jnp.where(full_lane == full_row, 0.5, 0.0))
            step = keep * change
            for precision in (coarse, coarse, precise):
                step = keep * (change - matmul(step, step, ((1,), (1,)), precision))
            weight = inverse
            for precision in (coarse, coarse, precise, precise):
                weight = inverse - matmul(step, weight, precision=precision)
            weight_ref[...] = weight
            triangle_ref[...] = upper + matmul(step, upper, ((0,), (0,)))

        @pl.when(jnp.logical_not(small))
        def _():
            a_ref[...] = change + eye
            eliminate(a_ref, y_ref, v_ref)
            weight_ref[...] = matmul(refined(y_ref[...], v_ref[...], eye), inverse)
            triangle_ref[...] = matmul(v_ref[...], upper)

    square = jax.ShapeDtypeStruct((size, size), jnp.float32)
    vmem = pl.BlockSpec(memory_space=pltpu.VMEM)
    return pl.pallas_call(
        kernel,
        in_specs=[pl.BlockSpec(memory_space=pltpu.SMEM), vmem, vmem],
        out_specs=[vmem, vmem, vmem],
        out_shape=[square, square, square],
        scratch_shapes=[pltpu.VMEM((size, size), jnp.float32)] * 5,
        name="factor",
    )(core, *[pltpu.with_memory_space_constraint(value, pltpu.VMEM) for value in (mine, other)])


def refined(inverse, upper, eye):
    return inverse + matmul(eye - matmul(inverse, upper, ((1,), (1,))), inverse)


def two_sum(left, right):
    total = left + right
    back = total - left
    return total, (left - (total - back)) + (right - back)


def gram_halves(parts, core, chunk=2048, piece=512):
    cells = parts[0].shape[1]
    count = len(parts)
    size = sum(rows_of(part) for part in parts)
    half, quarter = size // 2, size // 4
    steps = cells // chunk

    def kernel(core_ref, *refs):
        part_refs = refs[:count]
        keep_ref, send_ref, high_ref, low_ref, cross_ref = refs[count:]
        step = pl.program_id(0)

        @pl.when(step == 0)
        def _():
            high_ref[...] = jnp.zeros_like(high_ref)
            low_ref[...] = jnp.zeros_like(low_ref)
            cross_ref[...] = jnp.zeros_like(cross_ref)

        for k in range(chunk // piece):
            block = jnp.concatenate([columns(ref, k * piece // LANES, piece // LANES) for ref in part_refs], 0)
            first, second, third, _ = split(block, jnp.max(jnp.abs(block), 1, keepdims=True))
            lhs = jnp.concatenate([first, second, third], 0).astype(jnp.bfloat16)
            part = lax.dot_general(
                lhs, lhs[: 2 * size], (((1,), (1,)), ((), ())), preferred_element_type=jnp.float32
            )
            high_ref[...], error = two_sum(high_ref[...], part[:size, :size])
            low_ref[...] += error + part[size : 2 * size, size:]
            cross_ref[...] += part[size : 2 * size, :size] + (part[2 * size :, :size] + part[2 * size :, size:])

        @pl.when(step == steps - 1)
        def _():
            cross = cross_ref[...]
            high_ref[...], low_ref[...] = two_sum(high_ref[...], low_ref[...] + (cross + cross.T))
            lane = lax.broadcasted_iota(jnp.int32, (half, size), 1)
            row = lax.broadcasted_iota(jnp.int32, (half, size), 0)
            lead = core_ref[0] == 0
            for k, ref in enumerate((high_ref, low_ref)):
                corner = ref[half:, :]
                base = jnp.where(lane < row, pltpu.roll(corner, half, 1), ref[:half, :])
                diagonal = jnp.sum(jnp.where(lane == row + half, corner, 0.0), 0, keepdims=True)
                extra = jnp.broadcast_to(diagonal, (8, size))
                low = jnp.concatenate([base[:quarter], extra], 0)
                high = jnp.concatenate([base[quarter:], extra], 0)
                keep_ref[k] = jnp.where(lead, low, high)
                send_ref[k] = jnp.where(lead, high, low)

    out = jax.ShapeDtypeStruct((2, quarter + 8, size), jnp.float32)
    spec = pl.BlockSpec((2, quarter + 8, size), lambda i: (0, 0, 0))
    return pl.pallas_call(
        kernel,
        grid=(steps,),
        in_specs=[
            pl.BlockSpec(memory_space=pltpu.SMEM),
            *[window(part, chunk // LANES, lambda i: i) for part in parts],
        ],
        out_specs=[spec, spec],
        out_shape=[out, out],
        scratch_shapes=[pltpu.VMEM((size, size), jnp.float32)] * 3,
        name="gram_halves",
    )(core, *parts)


def apply_split(weight, parts, nx, nz, ny):
    count = sum(rows_of(part) for part in parts)
    halves = ny // LANES

    def kernel(w_ref, *refs):
        part_refs, out_ref = refs[:-1], refs[-1]
        w1, w2, w3 = three_parts(w_ref[...])
        lhs = jnp.concatenate(
            [
                jnp.concatenate([w1, w2], 1),
                jnp.concatenate([w2, w1], 1),
                jnp.concatenate([w3, jnp.zeros_like(w3)], 1),
            ],
            0,
        ).astype(jnp.bfloat16)
        block = jnp.concatenate([columns(ref, 0, nz) for ref in part_refs], 0)
        s1, s2, s3 = three_parts(block)
        pair = jnp.concatenate([s1, s2], 0).astype(jnp.bfloat16)
        dims = (((1,), (0,)), ((), ()))
        main = lax.dot_general(lhs, pair, dims, preferred_element_type=jnp.float32)
        tail = lax.dot_general(w1.astype(jnp.bfloat16), s3.astype(jnp.bfloat16), dims, preferred_element_type=jnp.float32)
        result = main[:count] + (main[count : 2 * count] + (main[2 * count :] + tail))
        flat = out_ref.reshape(count * nz, LANES)
        for z in range(nz):
            flat[pl.ds(z, count, stride=nz), :] = result[:, z * LANES : (z + 1) * LANES]

    return pl.pallas_call(
        kernel,
        grid=(nx, halves),
        in_specs=[
            pl.BlockSpec((count, count), lambda i, h: (0, 0)),
            *[window(part, nz, lambda i, h: i * halves + h) for part in parts],
        ],
        out_specs=pl.BlockSpec((count, 1, nz, LANES), lambda i, h: (0, i, 0, h)),
        out_shape=jax.ShapeDtypeStruct((count, nx, nz, ny), jnp.float32),
        name="apply_split",
    )(weight, *parts)


def shifted(value, axis, forward):
    count = lax.axis_size(axis)
    step = 1 if forward else count - 1
    return lax.ppermute(value, axis, [(i, (i + step) % count) for i in range(count)])


def flipped(value, flip_x, flip_z):
    size_x, size_z = lax.axis_size("gx"), lax.axis_size("gz")
    pairs = [
        (x * size_z + z, (x ^ flip_x) * size_z + (z ^ flip_z)) for x in range(size_x) for z in range(size_z)
    ]
    return lax.ppermute(value, ("gx", "gz"), pairs)


def pair_sum(left, right):
    high, error = two_sum(left[0], right[0])
    return jnp.stack([high, left[1] + right[1] + error])


def all_sum(keep, send):
    value = pair_sum(keep, flipped(send, 1, 0))
    flips = [(2, 0), (6, 0), (8, 0), (24, 0), (0, 1), (0, 2), (0, 6)]
    for flip_x, flip_z in flips:
        value = pair_sum(value, flipped(value, flip_x, flip_z))
    return value, flipped(value, 1, 0)


def shards(velocity, scaled_modes):
    _, _, cells_x, cells_z, cells_y = velocity.shape
    total_cells = cells_x * lax.axis_size("gx") * cells_z * lax.axis_size("gz") * cells_y
    core = (lax.axis_index("gx") % 2).astype(jnp.int32).reshape(1)
    halos = []
    for begin, count in SPANS:
        first_x, last_x, first_z, last_z = pack_faces(velocity, begin, count)
        low_x = shifted(last_x, "gx", True)
        high_x = shifted(first_x, "gx", False)
        low_z = shifted(last_z, "gz", True)
        high_z = shifted(first_z, "gz", False)
        halos.append((low_x, high_x, low_z, high_z))
    parts = [flatten_modes(scaled_modes)]
    for (begin, _), halo in zip(SPANS, halos):
        parts.append(criterion(velocity, *halo, begin))
    mine, other = all_sum(*gram_halves(parts, core))
    weight, triangle, lower_one = factor(mine, other, core, float(total_cells))
    basis = apply_split(weight, parts, cells_x, cells_z, cells_y)
    return basis, triangle, lower_one


def solution(mesh):
    in_specs = (P(None, None, "gx", "gz", None), P(None, "gx", "gz", None))
    out_specs = (P(None, "gx", "gz", None), P(), P())
    return jax.shard_map(shards, mesh=mesh, in_specs=in_specs, out_specs=out_specs, check_vma=False)
```

```python
import jax
import jax.numpy as jnp
from jax import lax
from jax.experimental import pallas as pl
from jax.experimental.pallas import tpu as pltpu
from jax.sharding import PartitionSpec as P


precise = lax.Precision.HIGHEST
coarse = lax.Precision.DEFAULT
LANES = 128
GRANT = 57 * 2**20
SPANS = ((0, 32), (32, 32))


def pack_faces(velocity, begin, snaps, group=16):
    _, comps, nx, nz, ny = velocity.shape
    skip = begin // group
    halves = ny // LANES
    rows = group * comps * nx

    def kernel(*refs):
        views, (first_x, last_x, first_z, last_z) = refs[:halves], refs[halves:]
        for h, v_ref in enumerate(views):
            lanes = slice(h * LANES, (h + 1) * LANES)
            first_x[:, :, :, lanes] = v_ref[:, :, 0]
            last_x[:, :, :, lanes] = v_ref[:, :, nx - 1]
            flat = v_ref.reshape(rows * nz, LANES)
            first_z[h] = flat[pl.ds(0, rows, stride=nz), :]
            last_z[h] = flat[pl.ds(nz - 1, rows, stride=nz), :]

    face_x = jax.ShapeDtypeStruct((snaps, comps, nz, ny), velocity.dtype)
    face_z = jax.ShapeDtypeStruct((halves, snaps * comps * nx, LANES), velocity.dtype)
    spec_x = pl.BlockSpec((group, comps, nz, ny), lambda i: (i, 0, 0, 0))
    spec_z = pl.BlockSpec((halves, rows, LANES), lambda i: (0, i, 0))
    block = (group, comps, nx, nz, LANES)
    return pl.pallas_call(
        kernel,
        grid=(snaps // group,),
        in_specs=[pl.BlockSpec(block, lambda i, h=h: (i + skip, 0, 0, 0, h)) for h in range(halves)],
        out_specs=[spec_x, spec_x, spec_z, spec_z],
        out_shape=[face_x, face_x, face_z, face_z],
        compiler_params=pltpu.CompilerParams(vmem_limit_bytes=GRANT),
        name="pack_faces",
    )(*[velocity] * halves)


def flatten_modes(modes, piece=512):
    count, nx, nz, ny = modes.shape
    halves = ny // LANES
    width = nx * nz * LANES

    def kernel(m_ref, out_ref, gram_ref):

        @pl.when(pl.program_id(0) == 0)
        def _():
            gram_ref[...] = jnp.zeros_like(gram_ref)

        flat = m_ref.reshape(count * nx * nz, LANES)
        for t in range(nx * nz):
            out_ref[:, t * LANES : (t + 1) * LANES] = flat[pl.ds(t, count, stride=nx * nz), :]
        for k in range(width // piece):
            block = out_ref[:, k * piece : (k + 1) * piece]
            first, second, third, _ = split(block, jnp.max(jnp.abs(block), 1, keepdims=True))
            lhs = jnp.concatenate([first, second, third], 0).astype(jnp.bfloat16)
            part = lax.dot_general(
                lhs, lhs[: 2 * count], (((1,), (1,)), ((), ())), preferred_element_type=jnp.float32
            )
            middle, last = part[count : 2 * count], part[2 * count :]
            gram_ref[0], error = two_sum(gram_ref[0], part[:count])
            gram_ref[1] += error + pltpu.roll(middle, count, 1)
            gram_ref[2] += middle + (last + pltpu.roll(last, count, 1))

    return pl.pallas_call(
        kernel,
        grid=(halves,),
        in_specs=[pl.BlockSpec((count, nx, nz, LANES), lambda h: (0, 0, 0, h))],
        out_specs=[
            pl.BlockSpec((count, width), lambda i: (0, i)),
            pl.BlockSpec((3, count, 2 * count), lambda i: (0, 0, 0)),
        ],
        out_shape=[
            jax.ShapeDtypeStruct((count, nx * nz * ny), modes.dtype),
            jax.ShapeDtypeStruct((3, count, 2 * count), jnp.float32),
        ],
        compiler_params=pltpu.CompilerParams(vmem_limit_bytes=GRANT),
        name="flatten_modes",
    )(modes)


def criterion(velocity, low_x, high_x, low_z, high_z, begin, group=8):
    _, comps, nx, nz, ny = velocity.shape
    snaps = low_x.shape[0]
    skip = begin // group
    halves = ny // LANES

    def kernel(v_ref, lx_ref, hx_ref, lz_ref, hz_ref, out_ref):
        flat = out_ref.reshape(nx * halves * nz * group, LANES)
        lane = lax.broadcasted_iota(jnp.int32, (nz, LANES), 1)
        level = lax.broadcasted_iota(jnp.int32, (nz, LANES), 0)

        def cut(half):
            return slice(half * LANES, (half + 1) * LANES)

        def wall(parts):
            below = [pltpu.roll(p, 1, 1) for p in parts]
            above = [pltpu.roll(p, LANES - 1, 1) for p in parts]
            out = []
            for h in range(halves):
                here = parts[h]
                fp = jnp.where(lane == LANES - 1, above[h + 1], above[h]) if h < halves - 1 else above[h]
                if h:
                    fm = jnp.where(lane == 0, below[h - 1], below[h])
                else:
                    edge = 3.0 * (here - fp) + pltpu.roll(here, LANES - 2, 1)
                    fm = jnp.where(lane == 0, edge, below[h])
                if h == halves - 1:
                    edge = 3.0 * (here - fm) + pltpu.roll(here, 2, 1)
                    fp = jnp.where(lane == LANES - 1, edge, fp)
                d = fp - fm
                out.append(d)
            return out

        def body(s, carry):
            t = pl.program_id(0) * group + s
            for x in range(nx):
                dx, dz, dy = [], [], []
                for c in range(comps):
                    here = [v_ref[s, c, x, :, cut(h)] for h in range(halves)]
                    dx.append([
                        (v_ref[s, c, x + 1, :, cut(h)] if x < nx - 1 else hx_ref[t, c, :, cut(h)])
                        - (v_ref[s, c, x - 1, :, cut(h)] if x else lx_ref[t, c, :, cut(h)])
                        for h in range(halves)
                    ])
                    row = (t * comps + c) * nx + x
                    part = []
                    for h in range(halves):
                        up = jnp.where(level == nz - 1, hz_ref.at[h][pl.ds(row, nz, stride=0), :], pltpu.roll(here[h], nz - 1, 0))
                        down = jnp.where(level == 0, lz_ref.at[h][pl.ds(row, nz, stride=0), :], pltpu.roll(here[h], 1, 0))
                        part.append(up - down)
                    dz.append(part)
                    dy.append(wall(here))
                for h in range(halves):
                    diagonal = dx[0][h] * dx[0][h] + dz[1][h] * dz[1][h] + dy[2][h] * dy[2][h]
                    cross = dz[0][h] * dx[1][h] + dy[0][h] * dx[2][h] + dy[1][h] * dz[2][h]
                    flat[pl.ds((h * nx + x) * nz * group + s, nz, stride=group), :] = -0.125 * diagonal - 0.25 * cross
            return carry

        lax.fori_loop(0, group, body, 0, unroll=4)

    near = pl.BlockSpec(memory_space=pltpu.VMEM)
    return pl.pallas_call(
        kernel,
        grid=(snaps // group,),
        in_specs=[pl.BlockSpec((group, comps, nx, nz, ny), lambda i: (i + skip, 0, 0, 0, 0)), near, near, near, near],
        out_specs=pl.BlockSpec((1, nx * halves * nz, group, LANES), lambda i: (i, 0, 0, 0)),
        out_shape=jax.ShapeDtypeStruct((snaps // group, nx * halves * nz, group, LANES), velocity.dtype),
        compiler_params=pltpu.CompilerParams(vmem_limit_bytes=GRANT),
        name="criterion",
    )(velocity, *[pltpu.with_memory_space_constraint(halo, pltpu.VMEM) for halo in (low_x, high_x, low_z, high_z)])


def columns(ref, begin, count):
    if len(ref.shape) == 2:
        return ref[:, begin * LANES : (begin + count) * LANES]
    return jnp.concatenate([ref[:, t].reshape(-1, LANES) for t in range(begin, begin + count)], 1)


def rows_of(part):
    return part.shape[0] if len(part.shape) == 2 else part.shape[0] * part.shape[2]


def window(part, count, index):
    if len(part.shape) == 2:
        return pl.BlockSpec((part.shape[0], count * LANES), lambda *ids: (0, index(*ids)))
    return pl.BlockSpec((part.shape[0], count, part.shape[2], LANES), lambda *ids: (0, index(*ids), 0, 0))


def spread(row, shape):
    return jnp.broadcast_to(row, shape)


def three_parts(value):
    first = value.astype(jnp.bfloat16).astype(jnp.float32)
    rest = value - first
    second = rest.astype(jnp.bfloat16).astype(jnp.float32)
    return first, second, rest - second


def eliminate(a_ref, x_ref, u_ref):
    size = a_ref.shape[0]
    tall = 8
    row = lax.broadcasted_iota(jnp.int32, (tall, size), 0)
    lane = lax.broadcasted_iota(jnp.int32, (tall, size), 1)
    full = (tall, size)
    full_row = lax.broadcasted_iota(jnp.int32, (size, size), 0)
    full_lane = lax.broadcasted_iota(jnp.int32, (size, size), 1)
    x_ref[...] = jnp.where(full_row == full_lane, 1.0, 0.0)
    for start in range(0, size, tall):
        rows = slice(start, start + tall)
        left, right = a_ref[rows, :], x_ref[rows, :]
        columns = [spread(left[:, start + j : start + j + 1], full) for j in range(tall)]
        pivots = jnp.ones(full, jnp.float32)
        for j in range(tall):
            pivot = spread(columns[j][j : j + 1, :], full)
            pivots = jnp.where(row == j, pivot, pivots)
            if j == tall - 1:
                break
            factor = jnp.where(row > j, columns[j] * (1.0 / pivot), 0.0)
            for k in range(j + 1, tall):
                columns[k] = columns[k] - factor * spread(columns[k][j : j + 1, :], full)
            left = left - factor * spread(left[j : j + 1, :], full)
            right = right - factor * spread(right[j : j + 1, :], full)
        scale = 1.0 / jnp.sqrt(pivots)
        left = jnp.where(lane >= start + row, left * scale, 0.0)
        right = right * scale
        u_ref[rows, :] = left
        x_ref[rows, :] = right
        if start + tall < size:
            l1, l2, l3 = three_parts(left)
            r1, r2, r3 = three_parts(right)
            lhs = jnp.concatenate([l1, l1, l2, l2, l1, l3], 0).astype(jnp.bfloat16)
            rhs_left = jnp.concatenate([l1, l2, l1, l2, l3, l1], 0).astype(jnp.bfloat16)
            rhs_right = jnp.concatenate([r1, r2, r1, r2, r3, r1], 0).astype(jnp.bfloat16)
            rhs = jnp.concatenate([rhs_left, rhs_right], 1)
            change = lax.dot_general(lhs, rhs, (((0,), (0,)), ((), ())), preferred_element_type=jnp.float32)
            below = slice(start + tall, size)
            a_ref[below, :] -= change[start + tall :, :size]
            x_ref[below, :] -= change[start + tall :, size:]


def matmul(left, right, dims=((1,), (0,)), precision=precise):
    return lax.dot_general(left, right, (dims, ((), ())), precision=precision, preferred_element_type=jnp.float32)


def split(value, top):
    big = top * (1.5 * 2.0**16)
    first = (value + big) - big
    rest = value - first
    second = rest.astype(jnp.bfloat16).astype(jnp.float32)
    rest = rest - second
    third = rest.astype(jnp.bfloat16).astype(jnp.float32)
    return first, second, third, rest - third


def residual(gram, upper):
    parts = [p.astype(jnp.bfloat16) for p in split(upper, jnp.max(jnp.abs(upper), 0, keepdims=True))]

    def cross(i, j):
        return lax.dot_general(parts[i], parts[j], (((0,), (0,)), ((), ())), preferred_element_type=jnp.float32)

    out = gram - cross(0, 0)
    both = cross(1, 0)
    out = out - (both + both.T)
    both = cross(2, 0) + (cross(3, 0) + cross(2, 1))
    return out - (cross(1, 1) + (both + both.T))


def factor(mine, other, core, cells):
    size = mine.shape[2]
    half = size // 2
    quarter = half // 2

    def kernel(core_ref, mine_ref, other_ref, weight_ref, triangle_ref, lower_ref, a_ref, x_ref, u_ref, y_ref, v_ref):
        full_row = lax.broadcasted_iota(jnp.int32, (size, size), 0)
        full_lane = lax.broadcasted_iota(jnp.int32, (size, size), 1)
        first = core_ref[0] == 0

        def whole(k):
            low = jnp.where(first, mine_ref[k], other_ref[k])
            high = jnp.where(first, other_ref[k], mine_ref[k])
            base = jnp.concatenate([low[:quarter], high[:quarter]], 0) * (1.0 / cells)
            diagonal = jnp.broadcast_to(low[quarter : quarter + 1] * (1.0 / cells), (size, size))
            rows = jnp.concatenate([base, pltpu.roll(base, half, 1)], 0)
            late = full_row >= half
            inside = jnp.logical_and(full_lane >= half, full_lane < full_row)
            own = jnp.logical_or(
                jnp.logical_and(jnp.logical_not(late), full_lane >= full_row), jnp.logical_and(late, inside)
            )
            rows = jnp.where(own, rows, rows.T)
            return jnp.where(jnp.logical_and(late, full_lane == full_row), diagonal, rows)

        gram, extra = whole(0), whole(1)
        a_ref[...] = gram
        eliminate(a_ref, x_ref, u_ref)
        upper = u_ref[...]
        eye = jnp.where(full_row == full_lane, 1.0, 0.0)
        inverse = refined(x_ref[...], upper, eye)
        lower_ref[...] = upper.T
        rest = residual(gram, upper) + extra
        change = matmul(matmul(inverse, rest), inverse, ((1,), (1,)))
        change = jnp.where(full_lane <= full_row, change, change.T)
        small = jnp.sum(change * change) < 2.0**-12

        @pl.when(small)
        def _():
            keep = jnp.where(full_lane < full_row, 1.0, jnp.where(full_lane == full_row, 0.5, 0.0))
            step = keep * change
            for precision in (coarse, coarse, precise):
                step = keep * (change - matmul(step, step, ((1,), (1,)), precision))
            weight = inverse
            for precision in (coarse, coarse, precise, precise):
                weight = inverse - matmul(step, weight, precision=precision)
            weight_ref[...] = weight
            triangle_ref[...] = upper + matmul(step, upper, ((0,), (0,)))

        @pl.when(jnp.logical_not(small))
        def _():
            a_ref[...] = change + eye
            eliminate(a_ref, y_ref, v_ref)
            weight_ref[...] = matmul(refined(y_ref[...], v_ref[...], eye), inverse)
            triangle_ref[...] = matmul(v_ref[...], upper)

    square = jax.ShapeDtypeStruct((size, size), jnp.float32)
    vmem = pl.BlockSpec(memory_space=pltpu.VMEM)
    return pl.pallas_call(
        kernel,
        in_specs=[pl.BlockSpec(memory_space=pltpu.SMEM), vmem, vmem],
        out_specs=[vmem, vmem, vmem],
        out_shape=[square, square, square],
        scratch_shapes=[pltpu.VMEM((size, size), jnp.float32)] * 5,
        name="factor",
    )(core, *[pltpu.with_memory_space_constraint(value, pltpu.VMEM) for value in (mine, other)])


def refined(inverse, upper, eye):
    return inverse + matmul(eye - matmul(inverse, upper, ((1,), (1,))), inverse)


def two_sum(left, right):
    total = left + right
    back = total - left
    return total, (left - (total - back)) + (right - back)


def gram_halves(parts, own, core, chunk=2048, piece=512):
    cells = parts[0].shape[1]
    count = len(parts)
    size = sum(rows_of(part) for part in parts)
    half, quarter = size // 2, size // 4
    steps = cells // chunk

    def kernel(core_ref, *refs):
        part_refs = refs[:count]
        own_ref, keep_ref, send_ref, high_ref, low_ref, cross_ref = refs[count:]
        side = lax.broadcasted_iota(jnp.int32, (half, size), 1) < half
        step = pl.program_id(0)

        @pl.when(step == 0)
        def _():
            high_ref[half:] = jnp.zeros((half, size), jnp.float32)
            low_ref[half:] = jnp.zeros((half, size), jnp.float32)
            cross_ref[half:] = jnp.zeros((half, size), jnp.float32)
            high_ref[:half] = own_ref[0]
            low_ref[:half] = own_ref[1]
            cross_ref[:half] = jnp.where(side, own_ref[2], 0.0)

        for k in range(chunk // piece):
            block = jnp.concatenate([columns(ref, k * piece // LANES, piece // LANES) for ref in part_refs], 0)
            first, second, third, _ = split(block, jnp.max(jnp.abs(block), 1, keepdims=True))
            lhs = jnp.concatenate([first[half:], second[half:], third[half:], third[:half]], 0).astype(jnp.bfloat16)
            rhs = jnp.concatenate([first, second], 0).astype(jnp.bfloat16)
            part = lax.dot_general(lhs, rhs, (((1,), (1,)), ((), ())), preferred_element_type=jnp.float32)
            top, middle, last = part[:half], part[half : 2 * half], part[2 * half : 3 * half]
            high_ref[half:], error = two_sum(high_ref[half:], top[:, :size])
            low_ref[half:] += error + middle[:, size:]
            cross_ref[half:] += (jnp.where(side, top[:, size:], 0.0) + middle[:, :size]) + (last[:, :size] + last[:, size:])
            cross_ref[:half] += jnp.where(side, 0.0, part[3 * half :, :size])

        @pl.when(step == steps - 1)
        def _():
            cross = cross_ref[...]
            high, low = two_sum(high_ref[...], low_ref[...] + (cross + cross.T))
            square_row = lax.broadcasted_iota(jnp.int32, (size, size), 0)
            square_lane = lax.broadcasted_iota(jnp.int32, (size, size), 1)
            mixed = jnp.logical_and(square_row < half, square_lane >= half)
            high_ref[...] = jnp.where(mixed, high.T, high)
            low_ref[...] = jnp.where(mixed, low.T, low)
            lane = lax.broadcasted_iota(jnp.int32, (half, size), 1)
            row = lax.broadcasted_iota(jnp.int32, (half, size), 0)
            lead = core_ref[0] == 0
            for k, ref in enumerate((high_ref, low_ref)):
                corner = ref[half:, :]
                base = jnp.where(lane < row, pltpu.roll(corner, half, 1), ref[:half, :])
                diagonal = jnp.sum(jnp.where(lane == row + half, corner, 0.0), 0, keepdims=True)
                extra = jnp.broadcast_to(diagonal, (8, size))
                low = jnp.concatenate([base[:quarter], extra], 0)
                high = jnp.concatenate([base[quarter:], extra], 0)
                keep_ref[k] = jnp.where(lead, low, high)
                send_ref[k] = jnp.where(lead, high, low)

    out = pltpu.VMEM((2, quarter + 8, size), jnp.float32)
    spec = pl.BlockSpec((2, quarter + 8, size), lambda i: (0, 0, 0))
    return pl.pallas_call(
        kernel,
        grid=(steps,),
        in_specs=[
            pl.BlockSpec(memory_space=pltpu.SMEM),
            *[window(part, chunk // LANES, lambda i: i) for part in parts],
            pl.BlockSpec((3, half, size), lambda i: (0, 0, 0)),
        ],
        out_specs=[spec, spec],
        out_shape=[out, out],
        scratch_shapes=[pltpu.VMEM((size, size), jnp.float32)] * 3,
        name="gram_halves",
    )(core, *parts, own)


def apply_split(weight, parts, nx, nz, ny, group=2):
    count = sum(rows_of(part) for part in parts)
    halves = ny // LANES

    def kernel(w_ref, *refs):
        part_refs, out_ref = refs[:-1], refs[-1]
        w1, w2, w3 = three_parts(w_ref[...])
        lhs = jnp.concatenate(
            [
                jnp.concatenate([w1, w2], 1),
                jnp.concatenate([w2, w1], 1),
                jnp.concatenate([w3, jnp.zeros_like(w3)], 1),
            ],
            0,
        ).astype(jnp.bfloat16)
        dims = (((1,), (0,)), ((), ()))
        flat = out_ref.reshape(count * group * nz, LANES)
        for x in range(group):
            block = jnp.concatenate([columns(ref, x * nz, nz) for ref in part_refs], 0)
            s1, s2, s3 = three_parts(block)
            pair = jnp.concatenate([s1, s2], 0).astype(jnp.bfloat16)
            main = lax.dot_general(lhs, pair, dims, preferred_element_type=jnp.float32)
            tail = lax.dot_general(
                w1.astype(jnp.bfloat16), s3.astype(jnp.bfloat16), dims, preferred_element_type=jnp.float32
            )
            result = main[:count] + (main[count : 2 * count] + (main[2 * count :] + tail))
            for z in range(nz):
                flat[pl.ds(x * nz + z, count, stride=group * nz), :] = result[:, z * LANES : (z + 1) * LANES]

    return pl.pallas_call(
        kernel,
        grid=(halves, nx // group),
        in_specs=[
            pl.BlockSpec((count, count), lambda h, i: (0, 0)),
            *[window(part, group * nz, lambda h, i: h * (nx // group) + i) for part in parts],
        ],
        out_specs=pl.BlockSpec((count, group, nz, LANES), lambda h, i: (0, i, 0, h)),
        out_shape=jax.ShapeDtypeStruct((count, nx, nz, ny), jnp.float32),
        name="apply_split",
    )(weight, *parts)


def shifted(value, axis, forward):
    count = lax.axis_size(axis)
    step = 1 if forward else count - 1
    return lax.ppermute(value, axis, [(i, (i + step) % count) for i in range(count)])


def flipped(value, flip_x, flip_z):
    size_x, size_z = lax.axis_size("gx"), lax.axis_size("gz")
    pairs = [
        (x * size_z + z, (x ^ flip_x) * size_z + (z ^ flip_z)) for x in range(size_x) for z in range(size_z)
    ]
    return lax.ppermute(value, ("gx", "gz"), pairs)


def pair_sum(left, right):
    high, error = two_sum(left[0], right[0])
    return jnp.stack([high, left[1] + right[1] + error])


def all_sum(keep, send):
    value = pair_sum(keep, flipped(send, 1, 0))
    flips = [(2, 0), (6, 0), (8, 0), (24, 0), (0, 1), (0, 2), (0, 6)]
    for flip_x, flip_z in flips:
        value = pair_sum(value, flipped(value, flip_x, flip_z))
    return value, flipped(value, 1, 0)


def shards(velocity, scaled_modes):
    _, _, cells_x, cells_z, cells_y = velocity.shape
    total_cells = cells_x * lax.axis_size("gx") * cells_z * lax.axis_size("gz") * cells_y
    core = (lax.axis_index("gx") % 2).astype(jnp.int32).reshape(1)
    halos = []
    for begin, count in SPANS:
        first_x, last_x, first_z, last_z = pack_faces(velocity, begin, count)
        low_x = shifted(last_x, "gx", True)
        high_x = shifted(first_x, "gx", False)
        low_z = shifted(last_z, "gz", True)
        high_z = shifted(first_z, "gz", False)
        halos.append((low_x, high_x, low_z, high_z))
    modes, own = flatten_modes(scaled_modes)
    parts = [modes]
    for (begin, _), halo in zip(SPANS, halos):
        parts.append(criterion(velocity, *halo, begin))
    mine, other = all_sum(*gram_halves(parts, own, core))
    weight, triangle, lower_one = factor(mine, other, core, float(total_cells))
    basis = apply_split(weight, parts, cells_x, cells_z, cells_y)
    return basis, triangle, lower_one


def solution(mesh):
    in_specs = (P(None, None, "gx", "gz", None), P(None, "gx", "gz", None))
    out_specs = (P(None, "gx", "gz", None), P(), P())
    return jax.shard_map(shards, mesh=mesh, in_specs=in_specs, out_specs=out_specs, check_vma=False)
```
